32 devices in a mesh: dp: 8 (over y, x, core), seq: 4 (over z).
Axes of the slice: x: 2, y: 2, z: 4, core: 2. Of those that a mesh axis runs over, the one named last changes fastest.
Arguments:
- tokens: bfloat16 [16, 1024, 1536], P('dp', 'seq'), may hold values from -6 to 6
- cotangent: bfloat16 [16, 1024, 1536], P('dp', 'seq'), may hold values from -6 to 6
- parents: int32 [16, 8], P('dp'), may hold values from 0 to 7, as said below
- adapter_ids: int32 [16], P('dp'), may hold values from 0 to 7
- attention_gain: float32 [1536], replicated, may hold values from 0.5 to 1.5
- mixer_weight: bfloat16 [1536, 6144], P('dp'), may hold values from -0.15625 to 0.15625
- forget_weight: bfloat16 [1536, 24], P('dp'), may hold values from -0.15625 to 0.15625
- forget_bias: float32 [24], replicated, may hold values from 1.5 to 8
- output_weight: bfloat16 [1536, 1536], P('dp'), may hold values from -1.75 to 1.75
- feedforward_gain: float32 [1536], replicated, may hold values from 0.5 to 1.5
- swiglu_weight: bfloat16 [1536, 8192], P('dp'), may hold values from -0.15625 to 0.15625
- down_weight: bfloat16 [4096, 1536], P('dp'), may hold values from -0.09375 to 0.09375
- adapter_inner: bfloat16 [8, 1536, 128], P(None, 'dp'), may hold values from -0.15625 to 0.15625
- adapter_hidden: bfloat16 [8, 4096, 16], P(None, 'dp'), may hold values from -0.09375 to 0.09375
- adapter_model: bfloat16 [8, 80, 1536], P(None, None, 'dp'), may hold values from -1.5 to 1.5
- adapter_project: bfloat16 [8, 16, 1536], P(None, None, 'dp'), may hold values from -4 to 4
- adapter_swiglu: bfloat16 [8, 32, 4096], P(None, None, 'dp'), may hold values from -1.5 to 1.5
- adapter_forget: bfloat16 [128, 24], P('dp'), may hold values from -1.5 to 1.5
Outputs:
- block_output: bfloat16 [16, 1024, 1536], P('dp', 'seq')
- tokens_grad: float32 [16, 1024, 1536], P('dp', 'seq')
- inner_grad: float32 [8, 1536, 128], P(None, 'dp')
- hidden_grad: float32 [8, 4096, 16], P(None, 'dp')
- model_grad: float32 [8, 80, 1536], P(None, None, 'dp')
- project_grad: float32 [8, 16, 1536], P(None, None, 'dp')
- swiglu_grad: float32 [8, 32, 4096], P(None, None, 'dp')
- forget_grad: float32 [128, 24], P('dp')
The draws below stay inside these ranges and needn't reach their ends.
Inputs may be any that keep to these rules, and one draw needn't show every extreme that they name: `parents`: in every row, entries 0 to 3 are 0, 0, 1, 2. Of blocks 4 to 7, two have parent 3, and each of the other two has one of those two as parent, a different one.
All inputs are finite; a program needn't handle non-finite values.
Results may differ from the reference program's by a relative error of at most 0.02.
Values may be sent and summed in bfloat16 or wider, within the bound.
A program may use at most 216 MiB of HBM per device.

```python
import jax
import jax.numpy as jnp
from jax import lax

D = 1536
H = 24
HD = 64
FF = 4096
RANK = 16
ADAPTERS = 8
BLOCK = 128
TREE_LEN = 1024
TREES = 16


def draw_parents(key, part):
    tree_keys = jax.random.split(key, TREES)
    orders = jax.vmap(lambda tree_key: jax.random.permutation(tree_key, 4))(tree_keys).astype(jnp.int32)
    places = orders + 4
    trunk_end = jnp.full((TREES,), 3, dtype=jnp.int32)
    upward = jnp.stack([trunk_end, trunk_end, places[:, 0], places[:, 1]], axis=1)
    slots = jnp.arange(4, 8, dtype=jnp.int32)
    chosen = (places[:, :, None] == slots[None, None, :]).astype(jnp.int32)
    tail = jnp.sum(chosen * upward[:, :, None], axis=1)
    trunk = jnp.broadcast_to(jnp.array([0, 0, 1, 2], dtype=jnp.int32), (TREES, 4))
    return jnp.concatenate([trunk, tail], axis=1).astype(jnp.int32)


def with_ends(values, key, low, top_value):
    longest = values.shape.index(max(values.shape))
    spots = []
    for shift in (0, 1):
        where = [jax.random.randint(jax.random.fold_in(key, axis), (), 0, length) for axis, length in enumerate(values.shape)]
        where[longest] = (where[longest] + shift) % values.shape[longest]
        spots.append(tuple(where))
    return values.at[spots[0]].set(low).at[spots[1]].set(top_value)


def steps_of(stream_key, shape, pieces, low, high):
    def one(axis_at, parts):
        steps = jax.random.uniform(jax.random.fold_in(jax.random.fold_in(stream_key, 6), axis_at), (parts,), jnp.float32, low / len(pieces), high / len(pieces))
        return jnp.repeat(jnp.exp(steps), shape[axis_at] // parts).reshape((-1,) + (1,) * (len(shape) - axis_at - 1))

    factor_of = one(*pieces[0])
    for cut in pieces[1:]:
        factor_of = factor_of * one(*cut)
    return factor_of


def noise(own_key, dims, width, most, cuts=(), kind=jnp.bfloat16):
    values = width * jax.random.normal(own_key, dims, jnp.float32)
    if cuts:
        values = values * steps_of(own_key, dims, cuts, -0.22, 0.18)
    return jnp.clip(values, -most, most).astype(kind)


def setup_inputs(seed: int = 0) -> dict:
    arg_keys = jax.random.split(jax.random.key(seed), 19)
    return {
        "tokens": noise(arg_keys[0], (TREES, TREE_LEN, D), 1.0, 6.0, ((0, 8), (1, 4))),
        "cotangent": noise(arg_keys[1], (TREES, TREE_LEN, D), 1.0, 6.0, ((0, 8), (1, 4))),
        "parents": draw_parents(jax.random.fold_in(arg_keys[18], 71), 0),
        "adapter_ids": with_ends(jax.random.randint(arg_keys[3], (TREES,), 0, ADAPTERS), jax.random.fold_in(arg_keys[3], 1), 0, ADAPTERS - 1).astype(jnp.int32),
        "attention_gain": jnp.clip(1.0 + 0.1 * jax.random.normal(arg_keys[4], (D,), jnp.float32), 0.5, 1.5),
        "mixer_weight": noise(arg_keys[5], (D, 4 * D), D ** -0.5, 0.15625, ((0, 8),)),
        "forget_weight": noise(arg_keys[6], (D, H), D ** -0.5, 0.15625, ((0, 8),)),
        "forget_bias": jnp.clip(jax.random.uniform(arg_keys[7], (H,), jnp.float32, 1.5, 8.0), 1.5, 8.0),
        "output_weight": noise(arg_keys[8], (D, D), (max(D // 128, 1)) ** -0.5, 1.75, ((0, 8),)),
        "feedforward_gain": jnp.clip(1.0 + 0.1 * jax.random.normal(arg_keys[9], (D,), jnp.float32), 0.5, 1.5),
        "swiglu_weight": noise(arg_keys[10], (D, 2 * FF), D ** -0.5, 0.15625, ((0, 8),)),
        "down_weight": noise(arg_keys[11], (FF, D), FF ** -0.5, 0.09375, ((0, 8),)),
        "adapter_inner": noise(arg_keys[12], (ADAPTERS, D, 8 * RANK), D ** -0.5, 0.15625, ((1, 8),)),
        "adapter_hidden": noise(arg_keys[13], (ADAPTERS, FF, RANK), FF ** -0.5, 0.09375, ((1, 8),)),
        "adapter_model": noise(arg_keys[14], (ADAPTERS, 5 * RANK, D), RANK ** -0.5, 1.5, ((2, 8),)),
        "adapter_project": noise(arg_keys[15], (ADAPTERS, RANK, D), (max(RANK // 8, 1)) ** -0.5, 4.0, ((2, 8),)),
        "adapter_swiglu": noise(arg_keys[16], (ADAPTERS, 2 * RANK, FF), RANK ** -0.5, 1.5, ((2, 8),)),
        "adapter_forget": noise(arg_keys[17], (ADAPTERS * RANK, H), RANK ** -0.5, 1.5, ((0, 8),)),
    }


@jax.custom_vjp
def low(v):
    return lax.optimization_barrier(v.astype(jnp.bfloat16)).astype(jnp.float32)

@jax.custom_vjp
def low_back(v):
    return v

def low_keep(v):
    return (low(v), None)

def low_pass(kept, grad):
    return (grad,)

def back_keep(v):
    return (v, None)

def back_low(kept, grad):
    return (low(grad),)
low.defvjp(low_keep, low_pass)
low_back.defvjp(back_keep, back_low)
highest = lax.Precision.HIGHEST
epsilon = 1e-06

def linear(left, right):
    return jnp.dot(left, right, precision=highest, preferred_element_type=jnp.float32)

def rms_norm(values, gain):
    return values * lax.rsqrt(lax.optimization_barrier(jnp.mean(values * values, axis=-1, keepdims=True)) + epsilon) * gain

def ancestry(parent_row):
    blocks = jnp.arange(8, dtype=jnp.int32)
    step_up = ((parent_row[:, None] == blocks[None, :]) & (blocks[:, None] != 0)).astype(jnp.float32)
    reach = jnp.eye(8, dtype=jnp.float32)
    power = reach
    for level in range(7):
        power = jnp.dot(power, step_up, precision=highest)
        reach = reach + power
    return reach

def tree_forward(inputs, parent_row, which, frozen, adapters):
    attention_gain, mixer_weight, forget_weight, forget_bias, output_weight, feedforward_gain, swiglu_weight, down_weight = frozen
    adapter_inner, adapter_hidden, adapter_model, adapter_project, adapter_swiglu, adapter_forget = adapters
    inner_sel = lax.dynamic_index_in_dim(adapter_inner, which, 0, keepdims=False)
    hidden_sel = lax.dynamic_index_in_dim(adapter_hidden, which, 0, keepdims=False)
    model_sel = lax.dynamic_index_in_dim(adapter_model, which, 0, keepdims=False)
    project_sel = lax.dynamic_index_in_dim(adapter_project, which, 0, keepdims=False)
    swiglu_sel = lax.dynamic_index_in_dim(adapter_swiglu, which, 0, keepdims=False)
    forget_sel = lax.dynamic_slice_in_dim(adapter_forget, which * RANK, RANK, 0)
    length = inputs.shape[0]
    first_norm = low(rms_norm(inputs, attention_gain))
    inner_low = low(low_back(linear(first_norm, inner_sel[:, :5 * RANK])))
    side = jnp.einsum('tpr,prd->tpd', inner_low[:, :4 * RANK].reshape(length, 4, RANK), model_sel[:4 * RANK].reshape(4, RANK, D), precision=highest)
    mix = low_back(linear(first_norm, mixer_weight) + side.reshape(length, 4 * D))
    queries = low(mix[:, :D])
    keys_all = low(mix[:, D:2 * D])
    values_all = low(mix[:, 2 * D:3 * D])
    gate_logit = mix[:, 3 * D:]
    forget_logit = low(low_back(linear(first_norm, forget_weight) + linear(inner_low[:, 4 * RANK:], forget_sel) + forget_bias))
    log_forget = jax.nn.log_sigmoid(forget_logit)
    positions = jnp.arange(length, dtype=jnp.int32)
    blocks = positions // BLOCK
    reach = ancestry(parent_row)
    picked = (blocks[:, None] == jnp.arange(8, dtype=jnp.int32)[None, :]).astype(jnp.float32)
    linked = linear(linear(picked, reach), picked.T)
    allowed = (linked > 0.5) & ((blocks[:, None] != blocks[None, :]) | (positions[None, :] <= positions[:, None]))
    path_sum = linear(allowed.astype(jnp.float32), log_forget).T
    scale = HD ** (-0.5)
    query_heads = queries.reshape(length, H, HD)
    key_heads = keys_all.reshape(length, H, HD)
    value_heads = values_all.reshape(length, H, HD)
    scores = jnp.einsum('thd,shd->hts', query_heads, key_heads, precision=highest) * scale
    scores = scores + path_sum[:, :, None] - path_sum[:, None, :]
    scores = low_back(jnp.where(allowed[None], scores, -1e+30))
    probs = jax.nn.softmax(scores, axis=2)
    attended = jnp.einsum('hts,shd->thd', low(probs), value_heads, precision=highest).reshape(length, D)
    attended = low_back(attended)
    gate_open = jax.nn.sigmoid(gate_logit)
    gated = low(attended * gate_open)
    project_low = low(low_back(linear(gated, inner_sel[:, 5 * RANK:6 * RANK])))
    middle = inputs + low_back(linear(gated, output_weight) + linear(project_low, project_sel))
    second_norm = low(rms_norm(middle, feedforward_gain))
    swiglu_low = low(low_back(linear(second_norm, inner_sel[:, 6 * RANK:])))
    lifted_side = jnp.einsum('tpr,prf->tpf', swiglu_low.reshape(length, 2, RANK), swiglu_sel.reshape(2, RANK, FF), precision=highest)
    lifted = low_back(linear(second_norm, swiglu_weight) + lifted_side.reshape(length, 2 * FF))
    activated = low(jax.nn.silu(lifted[:, :FF]) * lifted[:, FF:])
    hidden_low = low(low_back(linear(activated, hidden_sel)))
    return middle + low_back(linear(activated, down_weight) + linear(hidden_low, model_sel[4 * RANK:]))

def reference(tokens, cotangent, parents, adapter_ids, attention_gain, mixer_weight, forget_weight, forget_bias, output_weight, feedforward_gain, swiglu_weight, down_weight, adapter_inner, adapter_hidden, adapter_model, adapter_project, adapter_swiglu, adapter_forget):
    frozen = (attention_gain.astype(jnp.float32), mixer_weight.astype(jnp.float32), forget_weight.astype(jnp.float32), forget_bias.astype(jnp.float32), output_weight.astype(jnp.float32), feedforward_gain.astype(jnp.float32), swiglu_weight.astype(jnp.float32), down_weight.astype(jnp.float32))
    adapters = (adapter_inner.astype(jnp.float32), adapter_hidden.astype(jnp.float32), adapter_model.astype(jnp.float32), adapter_project.astype(jnp.float32), adapter_swiglu.astype(jnp.float32), adapter_forget.astype(jnp.float32))

    def per_tree(accum, packed):
        tree_tokens, tree_cotangent, parent_row, which = packed

        def forward(inputs, adapters_in):
            return tree_forward(inputs, parent_row, which, frozen, adapters_in)
        result, pullback = jax.vjp(forward, tree_tokens.astype(jnp.float32), adapters)
        input_grad, adapter_grads = pullback(tree_cotangent.astype(jnp.float32))
        accum = jax.tree.map(lambda total, piece: total + piece, accum, adapter_grads)
        return (accum, (result.astype(jnp.bfloat16), input_grad))
    zeros = jax.tree.map(jnp.zeros_like, adapters)
    accum, (outputs, input_grads) = lax.scan(per_tree, zeros, (tokens, cotangent, parents, adapter_ids))
    return (outputs, input_grads, accum[0], accum[1], accum[2], accum[3], accum[4], accum[5])
```

```python
import functools

import jax
import jax.numpy as jnp
from jax import lax
from jax.experimental import pallas as pl
from jax.experimental.pallas import tpu as pltpu
from jax.sharding import PartitionSpec as P

D = 1536
H = 24
HD = 64
FF = 4096
RANK = 16
ADAPTERS = 8
BLOCK = 128
TREE_LEN = 1024
EXTRA = 128
PAIRS = H // 2

ENTRIES = (2, 4, 6, 6)
FIRST = (0, 2, 6, 12)
TOTAL = 18

highest = lax.Precision.HIGHEST
epsilon = 1e-06
bf16 = jnp.bfloat16
f32 = jnp.float32


def linear(left, right):
    return jnp.dot(left, right, preferred_element_type=f32)


def linear_back(left, right):
    return lax.dot_general(left, right, (((1,), (1,)), ((), ())), preferred_element_type=f32)


def linear_grad(left, right):
    return lax.dot_general(left, right, (((0,), (0,)), ((), ())), preferred_element_type=f32)


def rms_scale(values):
    return lax.rsqrt(jnp.mean(values * values, axis=-1, keepdims=True) + epsilon)


def norm_back(values, gain, upstream):
    scale_rows = rms_scale(values)
    unit = values * scale_rows
    inner = upstream * gain
    return scale_rows * (inner - unit * jnp.mean(inner * unit, axis=-1, keepdims=True))


def attend_kernel(where_ref, q_ref, k_ref, v_ref, k2_ref, v2_ref, bias_ref, o_ref, p_ref, kbuf, vbuf):
    half = 4 * BLOCK
    kbuf[:half] = k_ref[...]
    kbuf[half:] = k2_ref[...]
    vbuf[:half] = v_ref[...]
    vbuf[half:] = v2_ref[...]
    lane = lax.broadcasted_iota(jnp.int32, (BLOCK, BLOCK), 1)
    row = lax.broadcasted_iota(jnp.int32, (BLOCK, BLOCK), 0)
    later = jnp.where(lane > row, f32(-1e30), f32(0.0))
    for place in range(4):
        count, first = ENTRIES[place], FIRST[place]
        queries = q_ref[place * BLOCK : (place + 1) * BLOCK, :]
        spots = [pl.multiple_of(where_ref[first + e] * BLOCK, BLOCK) for e in range(count)]
        keys = jnp.concatenate([kbuf[pl.ds(s, BLOCK), :] for s in spots], axis=0)
        values = jnp.concatenate([vbuf[pl.ds(s, BLOCK), :] for s in spots], axis=0)
        outs = []
        for a in range(2):
            mine = jnp.where((lane < HD) == (a == 0), queries, jnp.zeros_like(queries))
            scores = linear_back(mine, keys) * (HD ** (-0.5))
            scores = scores + bias_ref[a : a + 1, first * BLOCK : (first + count) * BLOCK]
            scores = jnp.concatenate(
                [scores[:, : (count - 1) * BLOCK], scores[:, (count - 1) * BLOCK :] + later], axis=1
            )
            peak = jnp.max(scores, axis=1, keepdims=True)
            expo = jnp.exp(scores - peak)
            total = jnp.sum(expo, axis=1, keepdims=True)
            probs = (expo * (1.0 / total)).astype(bf16)
            p_ref[a, :, first * BLOCK : (first + count) * BLOCK] = probs
            outs.append(linear(probs, values))
        o_ref[place * BLOCK : (place + 1) * BLOCK, :] = jnp.where(lane < HD, outs[0], outs[1])


def attend(where, queries, keys, values, keys2, values2, bias):
    rows = pl.BlockSpec((4 * BLOCK, 2 * HD), lambda g, w: (0, g))
    return pl.pallas_call(
        attend_kernel,
        out_shape=(
            jax.ShapeDtypeStruct((4 * BLOCK, D), f32),
            jax.ShapeDtypeStruct((H, BLOCK, TOTAL * BLOCK), bf16),
        ),
        grid_spec=pltpu.PrefetchScalarGridSpec(
            num_scalar_prefetch=1,
            grid=(PAIRS,),
            in_specs=[rows] * 5 + [pl.BlockSpec((None, 2, TOTAL * BLOCK), lambda g, w: (g, 0, 0))],
            out_specs=(rows, pl.BlockSpec((2, BLOCK, TOTAL * BLOCK), lambda g, w: (g, 0, 0))),
            scratch_shapes=[pltpu.VMEM((8 * BLOCK, 2 * HD), bf16)] * 2,
        ),
        cost_estimate=pl.CostEstimate(flops=8_000_000_000, bytes_accessed=25_000_000, transcendentals=7_000_000),
        name="attend",
    )(where, queries, keys, values, keys2, values2, bias)


def attend_back_kernel(
    where_ref, q_ref, k_ref, v_ref, k2_ref, v2_ref, g_ref, o_ref, p_ref,
    dq_ref, dk_ref, dv_ref, qsum_ref, ksum_ref, kbuf, vbuf, dkbuf, dvbuf,
):
    half = 4 * BLOCK
    pair = pl.program_id(0)
    kbuf[:half] = k_ref[...]
    kbuf[half:] = k2_ref[...]
    vbuf[:half] = v_ref[...]
    vbuf[half:] = v2_ref[...]
    dkbuf[...] = jnp.zeros_like(dkbuf)
    dvbuf[...] = jnp.zeros_like(dvbuf)
    ksum_ref[...] = jnp.zeros_like(ksum_ref)

    @pl.when(pair == 0)
    def _():
        qsum_ref[...] = jnp.zeros_like(qsum_ref)

    lane = lax.broadcasted_iota(jnp.int32, (BLOCK, BLOCK), 1)
    scale = HD ** (-0.5)
    for place in range(4):
        count, first = ENTRIES[place], FIRST[place]
        span = slice(place * BLOCK, (place + 1) * BLOCK)
        queries = q_ref[span, :]
        grads = g_ref[span, :]
        product = grads.astype(f32) * o_ref[span, :]
        spots = [pl.multiple_of(where_ref[first + e] * BLOCK, BLOCK) for e in range(count)]
        keys = jnp.concatenate([kbuf[pl.ds(s, BLOCK), :] for s in spots], axis=0)
        values = jnp.concatenate([vbuf[pl.ds(s, BLOCK), :] for s in spots], axis=0)
        dqs, dks, dvs = [], [], []
        row_sums = qsum_ref[span, :]
        for a in range(2):
            own = (lane < HD) == (a == 0)
            dot_row = jnp.sum(jnp.where(own, product, 0.0), axis=1, keepdims=True)
            mine = jnp.where(own, grads, jnp.zeros_like(grads))
            probs = p_ref[a, :, first * BLOCK : (first + count) * BLOCK]
            prob_grad = linear_back(mine, values)
            score_grad = (probs.astype(f32) * (prob_grad - dot_row)).astype(bf16)
            wide = score_grad.astype(f32)
            col = jnp.sum(wide, axis=0, keepdims=True)
            for e in range(count):
                ksum_ref[where_ref[first + e], a : a + 1, :] += col[:, e * BLOCK : (e + 1) * BLOCK]
            row_sums = row_sums + jnp.where(lane == 2 * pair + a, jnp.sum(wide, axis=1, keepdims=True), 0.0)
            dqs.append(linear(score_grad, keys))
            dks.append(linear_grad(score_grad, queries))
            dvs.append(linear_grad(probs, grads))
        qsum_ref[span, :] = row_sums
        dq_ref[span, :] = (jnp.where(lane < HD, dqs[0], dqs[1]) * scale).astype(bf16)
        for e in range(count):
            part = slice(e * BLOCK, (e + 1) * BLOCK)
            dkbuf[pl.ds(spots[e], BLOCK), :] += jnp.where(lane < HD, dks[0][part], dks[1][part])
            dvbuf[pl.ds(spots[e], BLOCK), :] += jnp.where(lane < HD, dvs[0][part], dvs[1][part])
    dk_ref[...] = (dkbuf[...] * scale).astype(bf16)
    dv_ref[...] = dvbuf[...].astype(bf16)


def attend_back(where, queries, keys, values, keys2, values2, grads, attended, probs):
    rows = pl.BlockSpec((4 * BLOCK, 2 * HD), lambda g, w: (0, g))
    full = pl.BlockSpec((8 * BLOCK, 2 * HD), lambda g, w: (0, g))
    return pl.pallas_call(
        attend_back_kernel,
        out_shape=(
            jax.ShapeDtypeStruct((4 * BLOCK, D), bf16),
            jax.ShapeDtypeStruct((8 * BLOCK, D), bf16),
            jax.ShapeDtypeStruct((8 * BLOCK, D), bf16),
            jax.ShapeDtypeStruct((4 * BLOCK, BLOCK), f32),
            jax.ShapeDtypeStruct((PAIRS, 8, 2, BLOCK), f32),
        ),
        grid_spec=pltpu.PrefetchScalarGridSpec(
            num_scalar_prefetch=1,
            grid=(PAIRS,),
            in_specs=[rows] * 7 + [pl.BlockSpec((2, BLOCK, TOTAL * BLOCK), lambda g, w: (g, 0, 0))],
            out_specs=(
                rows,
                full,
                full,
                pl.BlockSpec((4 * BLOCK, BLOCK), lambda g, w: (0, 0)),
                pl.BlockSpec((None, 8, 2, BLOCK), lambda g, w: (g, 0, 0, 0)),
            ),
            scratch_shapes=[pltpu.VMEM((8 * BLOCK, 2 * HD), bf16)] * 2
            + [pltpu.VMEM((8 * BLOCK, 2 * HD), f32)] * 2,
        ),
        cost_estimate=pl.CostEstimate(flops=16_000_000_000, bytes_accessed=35_000_000, transcendentals=0),
        name="attend_back",
    )(where, queries, keys, values, keys2, values2, grads, attended, probs)


def forward_kernel(x_ref, low_ref, w_ref, e_ref, b_ref, o_ref):
    out = linear(x_ref[...], w_ref[...]) + linear(low_ref[...], e_ref[...])
    o_ref[...] = (out + b_ref[...]).astype(o_ref.dtype)


def forward_mm(x, low, weight, extra, bias, first, count, width, dtype):
    rows, depth = x.shape
    whole = lambda v: pl.BlockSpec(v.shape, lambda j: (0,) * v.ndim)
    cols = lambda height: pl.BlockSpec((height, width), lambda j: (0, first + j))
    return pl.pallas_call(
        forward_kernel,
        out_shape=jax.ShapeDtypeStruct((rows, count * width), dtype),
        grid=(count,),
        in_specs=[whole(x), whole(low), cols(depth), cols(EXTRA), cols(1)],
        out_specs=pl.BlockSpec((rows, width), lambda j: (0, j)),
        cost_estimate=pl.CostEstimate(
            flops=2 * rows * (depth + EXTRA) * count * width,
            bytes_accessed=2 * depth * count * width + 2 * rows * depth,
            transcendentals=0,
        ),
        name="forward_mm",
    )(x, low, weight, extra, bias)


def backward_kernel(g_ref, w_ref, e_ref, acc_ref, acclow_ref, o_ref, low_ref):
    @pl.when(pl.program_id(0) == 0)
    def _():
        o_ref[...] = acc_ref[...]
        low_ref[...] = acclow_ref[...]

    grads = g_ref[...]
    o_ref[...] += linear_back(grads, w_ref[...])
    low_ref[...] += linear_back(grads, e_ref[...])


def backward_mm(g, weight, extra, first, count, width, acc, acc_low):
    rows = g.shape[0]
    depth = weight.shape[0]
    whole = lambda v: pl.BlockSpec(v.shape, lambda j: (0,) * v.ndim)
    cols = lambda height: pl.BlockSpec((height, width), lambda j: (0, first + j))
    return pl.pallas_call(
        backward_kernel,
        out_shape=(jax.ShapeDtypeStruct((rows, depth), f32), jax.ShapeDtypeStruct((rows, EXTRA), f32)),
        grid=(count,),
        in_specs=[
            pl.BlockSpec((rows, width), lambda j: (0, j)), cols(depth), cols(EXTRA), whole(acc), whole(acc_low)
        ],
        out_specs=(whole(acc), whole(acc_low)),
        cost_estimate=pl.CostEstimate(
            flops=2 * rows * (depth + EXTRA) * count * width,
            bytes_accessed=2 * depth * count * width + 8 * rows * depth,
            transcendentals=0,
        ),
        name="backward_mm",
    )(g, weight, extra, acc, acc_low)


def swiglu_kernel(
    x_ref, lowg_ref, lowu_ref, dy_ref, hlg_ref, g_ref, u_ref, bg_ref, bu_ref, dn_ref, ah_ref,
    second_ref, down_ref, slg_ref, slu_ref, hl_ref, pack_ref,
):
    @pl.when(pl.program_id(0) == 0)
    def _():
        for ref in (second_ref, down_ref, slg_ref, slu_ref, hl_ref):
            ref[...] = jnp.zeros_like(ref)

    gate = linear(x_ref[...], g_ref[...]) + linear(lowg_ref[...], bg_ref[...])
    up = linear(x_ref[...], u_ref[...]) + linear(lowu_ref[...], bu_ref[...])
    back = linear_back(dy_ref[...], dn_ref[...]) + linear(hlg_ref[...], ah_ref[...])
    sig = jax.nn.sigmoid(gate)
    silu = gate * sig
    activated = (silu * up).astype(bf16)
    gate_grad = (back * up * (sig * (1.0 + gate * (1.0 - sig)))).astype(bf16)
    up_grad = (back * silu).astype(bf16)
    down_ref[...] += linear(activated, dn_ref[...])
    hl_ref[...] += linear_back(activated, ah_ref[...])
    second_ref[...] += linear_back(gate_grad, g_ref[...]) + linear_back(up_grad, u_ref[...])
    slg_ref[...] += linear_back(gate_grad, bg_ref[...])
    slu_ref[...] += linear_back(up_grad, bu_ref[...])
    pack_ref[:RANK] = linear_grad(hlg_ref[...], activated).astype(bf16)
    pack_ref[RANK : 2 * RANK] = linear_grad(lowg_ref[...], gate_grad).astype(bf16)
    pack_ref[2 * RANK :] = linear_grad(lowu_ref[...], up_grad).astype(bf16)


def swiglu(x, lowg, lowu, dy, hlg, weight, bg, bu, down, ah):
    rows = x.shape[0]
    width = 512
    steps = FF // width
    whole = lambda v: pl.BlockSpec(v.shape, lambda j: (0,) * v.ndim)
    low = pl.BlockSpec((RANK, width), lambda j: (0, j))
    state = [jax.ShapeDtypeStruct((rows, n), f32) for n in (D, D, RANK, RANK, RANK)]
    return pl.pallas_call(
        swiglu_kernel,
        out_shape=tuple(state) + (jax.ShapeDtypeStruct((3 * RANK, FF), bf16),),
        grid=(steps,),
        in_specs=[whole(v) for v in (x, lowg, lowu, dy, hlg)]
        + [
            pl.BlockSpec((D, width), lambda j: (0, j)),
            pl.BlockSpec((D, width), lambda j: (0, steps + j)),
            low,
            low,
            pl.BlockSpec((width, D), lambda j: (j, 0)),
            low,
        ],
        out_specs=tuple(whole(v) for v in state) + (pl.BlockSpec((3 * RANK, width), lambda j: (0, j)),),
        cost_estimate=pl.CostEstimate(
            flops=12 * rows * D * FF, bytes_accessed=6 * D * FF + 24 * rows * D, transcendentals=rows * FF
        ),
        name="swiglu",
    )(x, lowg, lowu, dy, hlg, weight, weight, bg, bu, down, ah)


MESH = pl.DeviceIdType.MESH


def facts_kernel(facts_ref, forget_ref, facts_all, forget_out, send, recv):
    me, z = lax.axis_index("dp"), lax.axis_index("seq")
    barrier = pltpu.get_barrier_semaphore()
    for m in range(1, 8):
        pl.semaphore_signal(barrier, inc=1, device_id=(me ^ m, z), device_id_type=MESH)
    pl.semaphore_wait(barrier, 7)
    copies = []
    for m in range(1, 8):
        for kind, (src, dst) in enumerate(((facts_ref, facts_all), (forget_ref, forget_out))):
            copies.append(
                pltpu.make_async_remote_copy(
                    src_ref=src,
                    dst_ref=dst.at[me],
                    send_sem=send.at[kind, m],
                    recv_sem=recv.at[kind, m],
                    device_id=(me ^ m, z),
                    device_id_type=MESH,
                )
            )
            copies[-1].start()
    local = [
        pltpu.make_async_copy(facts_ref, facts_all.at[me], send.at[0, 0]),
        pltpu.make_async_copy(forget_ref, forget_out.at[me], send.at[1, 0]),
    ]
    for copy in local:
        copy.start()
    for copy in copies + local:
        copy.wait()


def share_facts(facts, forget):
    vmem = pl.BlockSpec(memory_space=pltpu.VMEM)
    return pl.pallas_call(
        facts_kernel,
        out_shape=(
            jax.ShapeDtypeStruct((8,) + facts.shape, facts.dtype),
            jax.ShapeDtypeStruct((8,) + forget.shape, forget.dtype),
        ),
        in_specs=[vmem, vmem],
        out_specs=(vmem, vmem),
        scratch_shapes=[pltpu.SemaphoreType.DMA((2, 8)), pltpu.SemaphoreType.DMA((2, 8))],
        compiler_params=pltpu.CompilerParams(collective_id=0, has_side_effects=True),
        name="share_facts",
    )(facts, forget)


def column_chunks(widths):
    chunks = []
    for index, (total, width) in enumerate(widths):
        for first in range(0, total, width):
            chunks.append((index, first, width))
    return chunks


def shared_rows(count):
    return count // 4


def gather_kernel(chunks, *refs):
    (tok, cot, inner, model, ffp, mix, fg, out, dn, sw) = refs[:10]
    (x_o, dy_o, inner_o, model_o, ff_o, mix_o, fg_o, out_o, dn_o, sw_o) = refs[10:20]
    send, recv, own_sem, small_send, small_recv, row_send, row_recv = refs[20:]
    me, z = lax.axis_index("dp"), lax.axis_index("seq")
    core, odd = me & 1, z & 1
    first_to = me ^ (2 + 2 * core)
    second_to = me ^ (4 - 2 * core)

    barrier = pltpu.get_barrier_semaphore()
    peers = [(me ^ m, z) for m in range(1, 8)] + [(me ^ m, z ^ k) for m in (0, 1) for k in (1, 2, 3)]
    for peer in peers:
        pl.semaphore_signal(barrier, inc=1, device_id=peer, device_id_type=MESH)
    pl.semaphore_wait(barrier, len(peers))

    sources = (mix, fg, out, dn, sw)
    targets = (mix_o, fg_o, out_o, dn_o, sw_o)
    done = []

    def remote(src, dst, s, r, to):
        copy = pltpu.make_async_remote_copy(
            src_ref=src, dst_ref=dst, send_sem=s, recv_sem=r, device_id=to, device_id_type=MESH
        )
        copy.start()
        done.append(copy)
        return copy

    tree_core = z >> 1
    rows = []
    for kind, (src, dst) in enumerate(((tok, x_o), (cot, dy_o))):
        for j in range(2):
            for b in range(2):
                to = ((me & ~1) | (b ^ odd), 2 * core + j)
                self_copy = (to[0] == me) & (to[1] == z)
                spot = dst.at[pl.ds(z * BLOCK, BLOCK)]
                far = pltpu.make_async_remote_copy(
                    src_ref=src.at[j, b],
                    dst_ref=spot,
                    send_sem=row_send.at[kind, 2 * j + b],
                    recv_sem=row_recv.at[kind, z],
                    device_id=to,
                    device_id_type=MESH,
                )
                near = pltpu.make_async_copy(src.at[j, b], spot, row_send.at[kind, 2 * j + b])

                @pl.when(self_copy)
                def _(near=near):
                    near.start()

                @pl.when(jnp.logical_not(self_copy))
                def _(far=far):
                    far.start()

                rows.append((self_copy, near, far))

    small = []
    for kind, (src, dst) in enumerate(((inner, inner_o), (model, model_o), (ffp, ff_o))):
        for m in range(1, 8):
            remote(src.at[me ^ m], dst.at[me], small_send.at[kind, m], small_recv.at[kind, m], (me ^ m, z))
        copy = pltpu.make_async_copy(src.at[me], dst.at[me], small_send.at[kind, 0])
        copy.start()
        small.append(copy)

    own = []
    for i, (index, first, width) in enumerate(chunks):
        src, dst = sources[index], targets[index]
        count = src.shape[0]
        copy = pltpu.make_async_copy(
            src.at[:, pl.ds(first, width)],
            dst.at[pl.ds(pl.multiple_of(me * count, count), count), pl.ds(first, width)],
            own_sem.at[i],
        )
        copy.start()
        own.append(copy)

    partner = (me ^ 1, z)
    above = (me, z ^ 1)
    state = {}

    def piece(i, owner, start, length):
        index, first, width = chunks[i]
        count = sources[index].shape[0]
        return targets[index].at[
            pl.ds(pl.multiple_of(owner * count + start, 16), length), pl.ds(first, width)
        ]

    def go(i, slot, src, dst, to):
        state[i, slot] = remote(src, dst, send.at[i, slot], recv.at[i, slot], to)

    def shape_of(i):
        index, first, width = chunks[i]
        count = sources[index].shape[0]
        shared = shared_rows(count)
        return count, shared, shared * odd, count - shared

    def pass_on(i, slot, owner, start, length, target):
        ref = piece(i, owner, start, length)
        go(i, slot, ref, ref, target)

    total = len(chunks)
    for i in range(total + 3):
        if i < total:
            index, first, width = chunks[i]
            count, shared, low, length = shape_of(i)
            src = sources[index].at[pl.ds(pl.multiple_of(low, 16), length), pl.ds(first, width)]
            go(i, 0, src, piece(i, me, low, length), (first_to, z))
            go(i, 1, src, piece(i, me, low, length), (second_to, z))
            go(i, 6, sources[index].at[:, pl.ds(first, width)], piece(i, me, 0, count), partner)
        k = i - 1
        if 0 <= k < total:
            count, shared, low, length = shape_of(k)
            state[k, 0].wait_recv()
            pass_on(k, 2, first_to, low, length, (second_to, z))
            pass_on(k, 7, first_to, low, length, partner)
            pass_on(k, 3, first_to, odd * (count - shared), shared, above)
            state[k, 1].wait_recv()
            pass_on(k, 8, second_to, low, length, partner)
            pass_on(k, 4, second_to, odd * (count - shared), shared, above)
        k = i - 2
        if 0 <= k < total:
            count, shared, low, length = shape_of(k)
            state[k, 2].wait_recv()
            pass_on(k, 9, me ^ 6, low, length, partner)
            pass_on(k, 5, me ^ 6, odd * (count - shared), shared, above)
        k = i - 3
        if 0 <= k < total:
            count, shared, low, length = shape_of(k)
            for n, owner in enumerate((first_to, second_to, me ^ 6)):
                state[k, 3 + n].wait_recv()
                pass_on(k, 10 + n, owner, (1 - odd) * (count - shared), shared, partner)
    for i in range(total):
        for slot in range(6, 13):
            state[i, slot].wait_recv()
    for copy in done:
        copy.wait_send()
    for kind in range(3):
        for m in range(7):
            done[kind * 7 + m].wait_recv()
    for copy in own + small:
        copy.wait()
    for self_copy, near, far in rows:
        @pl.when(self_copy)
        def _(near=near):
            near.wait()

        @pl.when(jnp.logical_not(self_copy))
        def _(far=far):
            far.wait_send()

    for kind, dst in enumerate((x_o, dy_o)):
        for p in range(4):
            from_me = (p == z) & (core == tree_core)
            arrived = pltpu.make_async_remote_copy(
                src_ref=tok.at[0, 0],
                dst_ref=dst.at[pl.ds(p * BLOCK, BLOCK)],
                send_sem=row_send.at[kind, p],
                recv_sem=row_recv.at[kind, p],
                device_id=(me ^ 1, z),
                device_id_type=MESH,
            )

            @pl.when(jnp.logical_not(from_me))
            def _(arrived=arrived):
                arrived.wait_recv()


def gather_all(tokens, cotangent, inner, model, ffp, mix, fg, out, dn, sw):
    chunks = column_chunks(((4 * D, 1024), (EXTRA, EXTRA), (D, D), (D, 512), (2 * FF, 1024)))
    vmem = pl.BlockSpec(memory_space=pltpu.VMEM)
    hbm = pl.BlockSpec(memory_space=pl.ANY)
    args = (tokens.reshape(2, 2, BLOCK, D), cotangent.reshape(2, 2, BLOCK, D), inner, model, ffp, mix, fg, out, dn, sw)
    n = len(chunks)
    shapes = [jax.ShapeDtypeStruct((4 * BLOCK, D), bf16)] * 2
    shapes += [jax.ShapeDtypeStruct(v.shape, bf16) for v in (inner, model, ffp)]
    shapes += [jax.ShapeDtypeStruct((8 * v.shape[0], v.shape[1]), bf16) for v in (mix, fg, out, dn, sw)]
    dma = pltpu.SemaphoreType.DMA
    return pl.pallas_call(
        functools.partial(gather_kernel, chunks),
        out_shape=tuple(shapes),
        in_specs=[vmem] * len(args),
        out_specs=(hbm,) * len(shapes),
        scratch_shapes=[dma((n, 13)), dma((n, 13)), dma((n,)), dma((3, 8)), dma((3, 8)), dma((2, 4)), dma((2, 4))],
        compiler_params=pltpu.CompilerParams(collective_id=1, has_side_effects=True),
        name="gather_all",
    )(*args)


def body(
    devices,
    tokens,
    cotangent,
    parents,
    adapter_ids,
    attention_gain,
    mixer_weight,
    forget_weight,
    forget_bias,
    output_weight,
    feedforward_gain,
    swiglu_weight,
    down_weight,
    adapter_inner,
    adapter_hidden,
    adapter_model,
    adapter_project,
    adapter_swiglu,
    adapter_forget,
):
    dp, seq = devices
    paired = dp == 8
    me = lax.axis_index("dp")
    z = lax.axis_index("seq")
    core = me & 1
    tree_core, tree_slot = z >> 1, z & 1
    rows = 4 * BLOCK
    wide = D // dp
    tall = FF // dp

    def swap(value, bit):
        return lax.ppermute(value, "dp", [(i, i ^ bit) for i in range(dp)])

    def routes(step):
        high, low = step >> 1, step & 1
        pairs = []
        for d in range(dp):
            for s in range(seq):
                slot = high ^ (s >> 1)
                target = ((d & ~1) | (low ^ (s & 1))) * seq + 2 * (d & 1) + slot
                pairs.append((d * seq + s, target))
        return pairs

    def spread(value):
        cut = value.reshape(2, 2, BLOCK, D)
        got = []
        for step in range(4):
            piece = lax.dynamic_index_in_dim(cut[:, step & 1], (step >> 1) ^ (z >> 1), 0, keepdims=False)
            got.append(lax.ppermute(piece, ("dp", "seq"), routes(step)))
        stacked = jnp.stack(got)
        order = [lax.dynamic_index_in_dim(stacked, p ^ (2 * tree_slot + core), 0, keepdims=False) for p in range(4)]
        return jnp.concatenate(order, axis=0)

    def collect(value):
        cut = value.reshape(4, BLOCK, D)
        got = []
        for step in range(4):
            piece = lax.dynamic_index_in_dim(cut, step ^ (2 * tree_slot + core), 0, keepdims=False)
            got.append(lax.ppermute(piece, ("dp", "seq"), [(b, a) for a, b in routes(step)]))
        stacked = jnp.stack(got).reshape(2, 2 * BLOCK, D)
        order = [lax.dynamic_index_in_dim(stacked, t ^ (z >> 1), 0, keepdims=False) for t in range(2)]
        return jnp.stack(order)

    def gather_small(value):
        bit = 1
        while bit < dp:
            other = swap(value, bit)
            flag = (me & bit) != 0
            value = jnp.concatenate([jnp.where(flag, other, value), jnp.where(flag, value, other)], axis=0)
            bit *= 2
        return value

    facts = jnp.concatenate([parents, adapter_ids[:, None]], axis=1)
    if paired:
        facts, forget_all = share_facts(jnp.pad(facts, ((0, 6), (0, 128 - 9))), jnp.pad(adapter_forget, ((0, 0), (0, EXTRA - H))))
        facts = facts[:, :2, :9].reshape(2 * dp, 9)
        forget_all = forget_all[:, :, :H].reshape(ADAPTERS * RANK, H)
    else:
        facts = gather_small(facts)
        forget_all = gather_small(adapter_forget)
    all_ids = facts[:, 8]
    tree = 2 * ((me & ~1) | tree_core) + tree_slot
    parent_row = lax.dynamic_index_in_dim(facts, tree, 0, keepdims=False)[:8]
    which = lax.dynamic_index_in_dim(all_ids, tree, 0, keepdims=False)

    def to_trees(value):
        sent = []
        for d in range(dp):
            owner_tree = 2 * ((d & ~1) | tree_core) + tree_slot
            chosen = lax.dynamic_index_in_dim(all_ids, owner_tree, 0, keepdims=False)
            sent.append(lax.dynamic_index_in_dim(value, chosen, 0, keepdims=False))
        return jnp.stack(sent)

    got_inner = to_trees(adapter_inner)
    got_model = to_trees(jnp.concatenate([adapter_model, adapter_project], axis=1))
    got_ff = to_trees(jnp.concatenate([jnp.swapaxes(adapter_hidden, 1, 2), adapter_swiglu], axis=1))
    padded_forget = jnp.pad(forget_weight, ((0, 0), (0, EXTRA - H)))
    shards = (mixer_weight, padded_forget, output_weight, down_weight, swiglu_weight)
    if paired:
        gathered = gather_all(tokens, cotangent, got_inner, got_model, got_ff, *shards)
        x, dy, got_inner, got_model, got_ff = gathered[:5]
        w_mix, w_forget, w_out, w_down, w_swiglu = gathered[5:]
    else:
        x, dy = spread(tokens), spread(cotangent)
        got_inner, got_model, got_ff = (
            lax.all_to_all(v, "dp", 0, 0, tiled=True) for v in (got_inner, got_model, got_ff)
        )
        w_mix, w_forget, w_out, w_down, w_swiglu = (lax.all_gather(v, "dp", axis=0, tiled=True) for v in shards)
    inner_sel = got_inner.reshape(D, 8 * RANK)
    model_sel = jnp.swapaxes(got_model, 0, 1).reshape(6 * RANK, D)
    ff_sel = jnp.swapaxes(got_ff, 0, 1).reshape(3 * RANK, FF)
    forget_sel = lax.dynamic_slice_in_dim(forget_all, which * RANK, RANK, 0)

    zero = functools.partial(jnp.zeros, dtype=bf16)
    b_q, b_k, b_v, b_g, b_down, b_project = (model_sel[i * RANK : (i + 1) * RANK] for i in range(6))
    none = zero((RANK, D))
    line = lambda *blocks: jnp.concatenate(blocks, axis=1)
    extra_mix = jnp.concatenate(
        [
            line(b_q, none, none, none),
            line(none, b_k, none, none),
            line(none, none, b_v, none),
            line(none, none, none, b_g),
            zero((EXTRA - 4 * RANK, 4 * D)),
        ],
        axis=0,
    )
    a_in = inner_sel[:, : 5 * RANK]
    a_project = inner_sel[:, 5 * RANK : 6 * RANK]
    a_swiglu = inner_sel[:, 6 * RANK :]
    inputs = x.astype(f32)
    first_norm = (inputs * rms_scale(inputs) * attention_gain).astype(bf16)
    inner_low = linear(first_norm, a_in).astype(bf16)
    group = lambda v, i: v[:, i * RANK : (i + 1) * RANK]
    pad_low = lambda v: jnp.pad(v, ((0, 0), (0, EXTRA - v.shape[1])))
    low_pad = pad_low(inner_low)
    zero_row = jnp.zeros((1, 4 * D), f32)
    mix = lambda first, count, dtype: forward_mm(first_norm, low_pad, w_mix, extra_mix, zero_row, first, count, 512, dtype)
    forget_logit = (
        linear(first_norm, w_forget)[:, :H] + linear(group(inner_low, 4), forget_sel) + forget_bias
    ).astype(bf16)
    kv = mix(3, 6, bf16)
    kv2 = swap(kv, 1)
    forget2 = swap(forget_logit, 1)
    keys, values = kv[:, :D], kv[:, D:]
    keys2, values2 = kv2[:, :D], kv2[:, D:]
    queries = mix(0, 3, bf16)
    gate_logit = mix(9, 3, f32)

    table = jnp.array([[0, 3, 4, 7], [1, 2, 5, 6]], dtype=jnp.int32)
    mine_ids = lax.dynamic_index_in_dim(table, core, 0, keepdims=False)
    ids = jnp.concatenate([mine_ids, lax.dynamic_index_in_dim(table, 1 - core, 0, keepdims=False)])
    block = jnp.arange(8, dtype=jnp.int32)
    trunk = (block[None, :] < 4) & (block[None, :] <= block[:, None])
    reach = trunk | (block[:, None] == block[None, :]) | (
        (block[:, None] >= 4) & (block[None, :] >= 4) & (parent_row[:, None] == block[None, :])
    )
    strict = (reach & (block[:, None] != block[None, :])).astype(f32)
    pick = (ids[:, None] == block[None, :]).astype(f32)
    strict_local = jnp.dot(jnp.dot(pick, strict, precision=highest), pick.T, precision=highest)
    spot_of = jnp.array([0, 4, 5, 1, 2, 6, 7, 3], dtype=jnp.int32) ^ (4 * core)
    first_entries = jnp.where(
        core == 0,
        jnp.array([-1, 0, 0, 1, 2, 3], dtype=jnp.int32),
        jnp.array([0, 1, 0, 1, -1, 2], dtype=jnp.int32),
    )
    tails = []
    for place in (2, 3):
        own = mine_ids[place]
        up = parent_row[own]
        up = jnp.where(up >= 4, up, -1)
        tails.append(jnp.concatenate([jnp.arange(4, dtype=jnp.int32), up[None], own[None]]))
    entries = jnp.concatenate([first_entries] + tails)
    valid = entries >= 0
    where = jnp.where(valid, spot_of[jnp.maximum(entries, 0)], 0).astype(jnp.int32)

    logits_all = jnp.concatenate([forget_logit, forget2], axis=0).astype(f32)
    log_forget = jax.nn.log_sigmoid(logits_all).T.reshape(H, 8, BLOCK)
    upper = (jnp.arange(BLOCK)[:, None] <= jnp.arange(BLOCK)[None, :]).astype(f32)
    within = jnp.dot(log_forget, upper, precision=highest)
    offsets = jnp.dot(within[:, :, BLOCK - 1], strict_local.T, precision=highest)
    path_sum = within + offsets[:, :, None]
    bias = jnp.where(valid[None, :, None], -path_sum[:, where], -1e30)
    bias = bias.reshape(PAIRS, 2, TOTAL * BLOCK)

    attended, probs = attend(where, queries, keys, values, keys2, values2, bias)
    gate_open = jax.nn.sigmoid(gate_logit)
    gated = (attended * gate_open).astype(bf16)
    project_low = linear(gated, a_project).astype(bf16)
    extra_out = jnp.pad(b_project, ((0, EXTRA - RANK), (0, 0)))
    out = forward_mm(gated, pad_low(project_low), w_out, extra_out, zero_row, 0, 3, 512, f32)
    middle = inputs + out
    second_norm = (middle * rms_scale(middle) * feedforward_gain).astype(bf16)
    swiglu_low = linear(second_norm, a_swiglu).astype(bf16)
    lowg, lowu = swiglu_low[:, :RANK], swiglu_low[:, RANK:]

    hidden_low_grad = linear_back(dy, b_down).astype(bf16)
    second_out, down_out, slg, slu, hidden_low, ff_pack = swiglu(
        second_norm, lowg, lowu, dy, hidden_low_grad, w_swiglu,
        ff_sel[RANK : 2 * RANK], ff_sel[2 * RANK :], w_down, ff_sel[:RANK],
    )
    hidden_low = hidden_low.astype(bf16)
    result = (middle + down_out + linear(hidden_low, b_down)).astype(bf16)
    outputs = collect(result)

    swiglu_low_grad = jnp.concatenate([slg, slu], axis=1).astype(bf16)
    second_grad = second_out + linear_back(swiglu_low_grad, a_swiglu)
    middle_grad = dy.astype(f32) + norm_back(middle, feedforward_gain, second_grad)
    branch_grad = middle_grad.astype(bf16)
    project_low_grad = linear_back(branch_grad, b_project).astype(bf16)
    none_low = jnp.zeros((rows, EXTRA), f32)
    gated_grad = backward_mm(
        branch_grad, w_out, zero((EXTRA, D)), 0, 3, 512, linear_back(project_low_grad, a_project), none_low
    )[0]
    attended_grad = (gated_grad * gate_open).astype(bf16)
    gate_logit_grad = (gated_grad * attended * gate_open * (1.0 - gate_open)).astype(bf16)

    first_out, first_low = backward_mm(
        gate_logit_grad, w_mix, extra_mix, 9, 3, 512, jnp.zeros((rows, D), f32), none_low
    )
    dq, dk_all, dv_all, query_sum, key_sum = attend_back(
        where, queries, keys, values, keys2, values2, attended_grad, attended, probs
    )
    theirs = jnp.concatenate([dk_all[rows:], dv_all[rows:]], axis=1)
    back = swap(theirs, 1)
    key_sum = jnp.transpose(key_sum, (0, 2, 1, 3)).reshape(H, 8, BLOCK)
    query_part = query_sum[:, :H].T.reshape(H, 4, BLOCK)
    decay = jnp.concatenate([query_part - key_sum[:, :4], -key_sum[:, 4:]], axis=1)
    other = swap(decay, 1)
    decay = decay + jnp.concatenate([other[:, 4:], other[:, :4]], axis=1)
    suffix = jnp.dot(decay[:, :4], upper.T, precision=highest)
    below = jnp.dot(jnp.sum(decay, axis=2), strict_local[:, :4], precision=highest)
    logf_grad = (suffix + below[:, :, None]).reshape(H, rows).T
    forget_grad_low = (logf_grad * jax.nn.sigmoid(-forget_logit.astype(f32))).astype(bf16)

    first_out, first_low = backward_mm(dq, w_mix, extra_mix, 0, 3, 512, first_out, first_low)
    dk = (dk_all[:rows].astype(f32) + back[:, :D].astype(f32)).astype(bf16)
    dv = (dv_all[:rows].astype(f32) + back[:, D:].astype(f32)).astype(bf16)
    first_out, first_low = backward_mm(
        jnp.concatenate([dk, dv], axis=1), w_mix, extra_mix, 3, 6, 512, first_out, first_low
    )
    inner_low_grad = jnp.concatenate(
        [first_low[:, : 4 * RANK], linear_back(forget_grad_low, forget_sel)], axis=1
    ).astype(bf16)
    first_grad = first_out + linear_back(inner_low_grad, a_in) + linear_back(pad_low(forget_grad_low), w_forget)
    input_grad = middle_grad + norm_back(inputs, attention_gain, first_grad)
    input_grads = collect(input_grad.astype(bf16)).astype(f32)

    def to_owners(value):
        taken = lax.all_to_all(value, "dp", 0, 0, tiled=True)
        trees = jnp.sum(taken.astype(f32).reshape((dp // 2, 2) + value.shape[1:]), axis=1).astype(bf16)
        if seq != 4:
            return lax.all_gather(trees, "seq", axis=0, tiled=True)
        found = [trees]
        for k in (1, 2, 3):
            found.append(lax.ppermute(trees, "seq", [(i, i ^ k) for i in range(4)]))
        return jnp.concatenate(found, axis=0)

    chip = jnp.arange(dp // 2, dtype=jnp.int32)
    at = jnp.arange(seq, dtype=jnp.int32)
    if seq == 4:
        at = at ^ z
    tree_of = 2 * (2 * chip[None, :] + (at >> 1)[:, None]) + (at & 1)[:, None]
    id_of = all_ids[tree_of.reshape(-1)]
    one_hot = (jnp.arange(ADAPTERS, dtype=jnp.int32)[:, None] == id_of[None, :]).astype(bf16)

    def by_adapter(value):
        return jnp.einsum("at,trc->arc", one_hot, value, preferred_element_type=f32)

    ff_pack = jnp.swapaxes(ff_pack.reshape(3 * RANK, dp, tall), 0, 1)
    ff_sum = by_adapter(to_owners(ff_pack))

    early_lhs = jnp.concatenate(
        [
            linear_grad(gated, project_low_grad),
            linear_grad(second_norm, swiglu_low_grad),
            linear_grad(dy, hidden_low),
            linear_grad(branch_grad, project_low),
            linear_grad(gate_logit_grad, group(inner_low, 3)),
        ],
        axis=1,
    )
    early = jnp.pad(early_lhs, ((0, 0), (0, 128 - 6 * RANK))).astype(bf16).reshape(dp, wide, 128)
    early_sum = by_adapter(to_owners(early))

    forget_piece = linear_grad(forget_grad_low, group(inner_low, 4))
    forget_piece = forget_piece.T
    late = jnp.concatenate(
        [
            linear_grad(first_norm, inner_low_grad),
            linear_grad(dq, group(inner_low, 0)),
            linear_grad(dk, group(inner_low, 1)),
            linear_grad(dv, group(inner_low, 2)),
        ],
        axis=1,
    ).astype(bf16)
    late_sum = by_adapter(to_owners(late.reshape(dp, wide, 128)))
    forget_sum = by_adapter(to_owners(jnp.broadcast_to(forget_piece.astype(bf16)[None], (dp, RANK, H))))

    turned = lambda v: jnp.swapaxes(v, 1, 2)
    at16 = lambda v, i: v[:, :, i * RANK : (i + 1) * RANK]
    per = ADAPTERS * RANK // dp
    return (
        outputs,
        input_grads,
        jnp.concatenate([late_sum[:, :, : 5 * RANK], early_sum[:, :, : 3 * RANK]], axis=2),
        turned(ff_sum[:, :RANK]),
        turned(
            jnp.concatenate([late_sum[:, :, 5 * RANK :], at16(early_sum, 5), at16(early_sum, 3)], axis=2)
        ),
        turned(at16(early_sum, 4)),
        ff_sum[:, RANK:],
        lax.dynamic_slice_in_dim(forget_sum.reshape(ADAPTERS * RANK, H), me * per, per, 0),
    )


def solution(mesh):
    placed = (
        P("dp", "seq", None),
        P("dp", "seq", None),
        P("dp", None),
        P("dp"),
        P(),
        P("dp", None),
        P("dp", None),
        P(),
        P("dp", None),
        P(),
        P("dp", None),
        P("dp", None),
        P(None, "dp", None),
        P(None, "dp", None),
        P(None, None, "dp"),
        P(None, None, "dp"),
        P(None, None, "dp"),
        P("dp", None),
    )
    return jax.shard_map(
        functools.partial(body, (mesh.shape["dp"], mesh.shape["seq"])),
        mesh=mesh,
        in_specs=placed,
        out_specs=(
            P("dp", "seq", None),
            P("dp", "seq", None),
            P(None, "dp", None),
            P(None, "dp", None),
            P(None, None, "dp"),
            P(None, None, "dp"),
            P(None, None, "dp"),
            P("dp", None),
        ),
        check_vma=False,
    )
```

```python
import functools

import jax
import jax.numpy as jnp
from jax import lax
from jax.experimental import pallas as pl
from jax.experimental.pallas import tpu as pltpu
from jax.sharding import PartitionSpec as P

D = 1536
H = 24
HD = 64
FF = 4096
RANK = 16
ADAPTERS = 8
BLOCK = 128
TREE_LEN = 1024
EXTRA = 128
PAIRS = H // 2

ENTRIES = (2, 4, 6, 6)
FIRST = (0, 2, 6, 12)
TOTAL = 18

highest = lax.Precision.HIGHEST
epsilon = 1e-06
bf16 = jnp.bfloat16
f32 = jnp.float32


def linear(left, right):
    return jnp.dot(left, right, preferred_element_type=f32)


def linear_back(left, right):
    return lax.dot_general(left, right, (((1,), (1,)), ((), ())), preferred_element_type=f32)


def linear_grad(left, right):
    return lax.dot_general(left, right, (((0,), (0,)), ((), ())), preferred_element_type=f32)


def rms_scale(values):
    return lax.rsqrt(jnp.mean(values * values, axis=-1, keepdims=True) + epsilon)


def norm_back(values, gain, upstream):
    scale_rows = rms_scale(values)
    unit = values * scale_rows
    inner = upstream * gain
    return scale_rows * (inner - unit * jnp.mean(inner * unit, axis=-1, keepdims=True))


def attend_kernel(where_ref, q_ref, k_ref, v_ref, k2_ref, v2_ref, bias_ref, o_ref, p_ref, kbuf, vbuf):
    half = 4 * BLOCK
    kbuf[:half] = k_ref[...]
    kbuf[half:] = k2_ref[...]
    vbuf[:half] = v_ref[...]
    vbuf[half:] = v2_ref[...]
    lane = lax.broadcasted_iota(jnp.int32, (BLOCK, BLOCK), 1)
    row = lax.broadcasted_iota(jnp.int32, (BLOCK, BLOCK), 0)
    later = jnp.where(lane > row, f32(-1e30), f32(0.0))
    for place in range(4):
        count, first = ENTRIES[place], FIRST[place]
        queries = q_ref[place * BLOCK : (place + 1) * BLOCK, :]
        spots = [pl.multiple_of(where_ref[first + e] * BLOCK, BLOCK) for e in range(count)]
        keys = jnp.concatenate([kbuf[pl.ds(s, BLOCK), :] for s in spots], axis=0)
        values = jnp.concatenate([vbuf[pl.ds(s, BLOCK), :] for s in spots], axis=0)
        outs = []
        for a in range(2):
            mine = jnp.where((lane < HD) == (a == 0), queries, jnp.zeros_like(queries))
            scores = linear_back(mine, keys) * (HD ** (-0.5))
            scores = scores + bias_ref[a : a + 1, first * BLOCK : (first + count) * BLOCK]
            scores = jnp.concatenate(
                [scores[:, : (count - 1) * BLOCK], scores[:, (count - 1) * BLOCK :] + later], axis=1
            )
            peak = jnp.max(scores, axis=1, keepdims=True)
            expo = jnp.exp(scores - peak)
            total = jnp.sum(expo, axis=1, keepdims=True)
            probs = (expo * (1.0 / total)).astype(bf16)
            p_ref[a, :, first * BLOCK : (first + count) * BLOCK] = probs
            outs.append(linear(probs, values))
        o_ref[place * BLOCK : (place + 1) * BLOCK, :] = jnp.where(lane < HD, outs[0], outs[1])


def attend(where, queries, keys, values, keys2, values2, bias):
    rows = pl.BlockSpec((4 * BLOCK, 2 * HD), lambda g, w: (0, g))
    return pl.pallas_call(
        attend_kernel,
        out_shape=(
            jax.ShapeDtypeStruct((4 * BLOCK, D), f32),
            jax.ShapeDtypeStruct((H, BLOCK, TOTAL * BLOCK), bf16),
        ),
        grid_spec=pltpu.PrefetchScalarGridSpec(
            num_scalar_prefetch=1,
            grid=(PAIRS,),
            in_specs=[rows] * 5 + [pl.BlockSpec((None, 2, TOTAL * BLOCK), lambda g, w: (g, 0, 0))],
            out_specs=(rows, pl.BlockSpec((2, BLOCK, TOTAL * BLOCK), lambda g, w: (g, 0, 0))),
            scratch_shapes=[pltpu.VMEM((8 * BLOCK, 2 * HD), bf16)] * 2,
        ),
        cost_estimate=pl.CostEstimate(flops=8_000_000_000, bytes_accessed=25_000_000, transcendentals=7_000_000),
        name="attend",
    )(where, queries, keys, values, keys2, values2, bias)


def attend_back_kernel(
    where_ref, q_ref, k_ref, v_ref, k2_ref, v2_ref, g_ref, o_ref, p_ref,
    dq_ref, dk_ref, dv_ref, qsum_ref, ksum_ref, kbuf, vbuf, dkbuf, dvbuf,
):
    half = 4 * BLOCK
    pair = pl.program_id(0)
    kbuf[:half] = k_ref[...]
    kbuf[half:] = k2_ref[...]
    vbuf[:half] = v_ref[...]
    vbuf[half:] = v2_ref[...]
    dkbuf[...] = jnp.zeros_like(dkbuf)
    dvbuf[...] = jnp.zeros_like(dvbuf)

    @pl.when(pair == 0)
    def _():
        qsum_ref[...] = jnp.zeros_like(qsum_ref)
        ksum_ref[...] = jnp.zeros_like(ksum_ref)

    lane = lax.broadcasted_iota(jnp.int32, (BLOCK, BLOCK), 1)
    scale = HD ** (-0.5)
    for place in range(4):
        count, first = ENTRIES[place], FIRST[place]
        span = slice(place * BLOCK, (place + 1) * BLOCK)
        queries = q_ref[span, :]
        grads = g_ref[span, :]
        product = grads.astype(f32) * o_ref[span, :]
        spots = [pl.multiple_of(where_ref[first + e] * BLOCK, BLOCK) for e in range(count)]
        keys = jnp.concatenate([kbuf[pl.ds(s, BLOCK), :] for s in spots], axis=0)
        values = jnp.concatenate([vbuf[pl.ds(s, BLOCK), :] for s in spots], axis=0)
        dqs, dks, dvs = [], [], []
        row_sums = qsum_ref[span, :]
        for a in range(2):
            own = (lane < HD) == (a == 0)
            dot_row = jnp.sum(jnp.where(own, product, 0.0), axis=1, keepdims=True)
            mine = jnp.where(own, grads, jnp.zeros_like(grads))
            probs = p_ref[a, :, first * BLOCK : (first + count) * BLOCK]
            prob_grad = linear_back(mine, values)
            score_grad = (probs.astype(f32) * (prob_grad - dot_row)).astype(bf16)
            wide = score_grad.astype(f32)
            col = jnp.sum(wide, axis=0, keepdims=True)
            for e in range(count):
                ksum_ref[where_ref[first + e], pl.ds(2 * pair + a, 1), :] += col[:, e * BLOCK : (e + 1) * BLOCK]
            row_sums = row_sums + jnp.where(lane == 2 * pair + a, jnp.sum(wide, axis=1, keepdims=True), 0.0)
            dqs.append(linear(score_grad, keys))
            dks.append(linear_grad(score_grad, queries))
            dvs.append(linear_grad(probs, grads))
        qsum_ref[span, :] = row_sums
        dq_ref[span, :] = (jnp.where(lane < HD, dqs[0], dqs[1]) * scale).astype(bf16)
        for e in range(count):
            part = slice(e * BLOCK, (e + 1) * BLOCK)
            dkbuf[pl.ds(spots[e], BLOCK), :] += jnp.where(lane < HD, dks[0][part], dks[1][part])
            dvbuf[pl.ds(spots[e], BLOCK), :] += jnp.where(lane < HD, dvs[0][part], dvs[1][part])
    dk_ref[...] = (dkbuf[...] * scale).astype(bf16)
    dv_ref[...] = dvbuf[...].astype(bf16)


def attend_back(where, queries, keys, values, keys2, values2, grads, attended, probs):
    rows = pl.BlockSpec((4 * BLOCK, 2 * HD), lambda g, w: (0, g))
    full = pl.BlockSpec((8 * BLOCK, 2 * HD), lambda g, w: (0, g))
    return pl.pallas_call(
        attend_back_kernel,
        out_shape=(
            jax.ShapeDtypeStruct((4 * BLOCK, D), bf16),
            jax.ShapeDtypeStruct((8 * BLOCK, D), bf16),
            jax.ShapeDtypeStruct((8 * BLOCK, D), bf16),
            jax.ShapeDtypeStruct((4 * BLOCK, BLOCK), f32),
            jax.ShapeDtypeStruct((8, BLOCK, BLOCK), f32),
        ),
        grid_spec=pltpu.PrefetchScalarGridSpec(
            num_scalar_prefetch=1,
            grid=(PAIRS,),
            in_specs=[rows] * 7 + [pl.BlockSpec((2, BLOCK, TOTAL * BLOCK), lambda g, w: (g, 0, 0))],
            out_specs=(
                rows,
                full,
                full,
                pl.BlockSpec((4 * BLOCK, BLOCK), lambda g, w: (0, 0)),
                pl.BlockSpec((8, BLOCK, BLOCK), lambda g, w: (0, 0, 0)),
            ),
            scratch_shapes=[pltpu.VMEM((8 * BLOCK, 2 * HD), bf16)] * 2
            + [pltpu.VMEM((8 * BLOCK, 2 * HD), f32)] * 2,
        ),
        cost_estimate=pl.CostEstimate(flops=16_000_000_000, bytes_accessed=35_000_000, transcendentals=0),
        name="attend_back",
    )(where, queries, keys, values, keys2, values2, grads, attended, probs)


def forward_kernel(x_ref, low_ref, w_ref, e_ref, b_ref, o_ref):
    out = linear(x_ref[...], w_ref[...]) + linear(low_ref[...], e_ref[...])
    o_ref[...] = (out + b_ref[...]).astype(o_ref.dtype)


def forward_mm(x, low, weight, extra, bias, first, count, width, dtype):
    rows, depth = x.shape
    whole = lambda v: pl.BlockSpec(v.shape, lambda j: (0,) * v.ndim)
    cols = lambda height: pl.BlockSpec((height, width), lambda j: (0, first + j))
    return pl.pallas_call(
        forward_kernel,
        out_shape=jax.ShapeDtypeStruct((rows, count * width), dtype),
        grid=(count,),
        in_specs=[whole(x), whole(low), cols(depth), cols(EXTRA), cols(1)],
        out_specs=pl.BlockSpec((rows, width), lambda j: (0, j)),
        cost_estimate=pl.CostEstimate(
            flops=2 * rows * (depth + EXTRA) * count * width,
            bytes_accessed=2 * depth * count * width + 2 * rows * depth,
            transcendentals=0,
        ),
        name="forward_mm",
    )(x, low, weight, extra, bias)


def backward_kernel(g_ref, w_ref, e_ref, acc_ref, acclow_ref, o_ref, low_ref):
    @pl.when(pl.program_id(0) == 0)
    def _():
        o_ref[...] = acc_ref[...]
        low_ref[...] = acclow_ref[...]

    grads = g_ref[...]
    o_ref[...] += linear_back(grads, w_ref[...])
    low_ref[...] += linear_back(grads, e_ref[...])


def backward_mm(g, weight, extra, first, count, width, acc, acc_low):
    rows = g.shape[0]
    depth = weight.shape[0]
    whole = lambda v: pl.BlockSpec(v.shape, lambda j: (0,) * v.ndim)
    cols = lambda height: pl.BlockSpec((height, width), lambda j: (0, first + j))
    return pl.pallas_call(
        backward_kernel,
        out_shape=(jax.ShapeDtypeStruct((rows, depth), f32), jax.ShapeDtypeStruct((rows, EXTRA), f32)),
        grid=(count,),
        in_specs=[
            pl.BlockSpec((rows, width), lambda j: (0, j)), cols(depth), cols(EXTRA), whole(acc), whole(acc_low)
        ],
        out_specs=(whole(acc), whole(acc_low)),
        cost_estimate=pl.CostEstimate(
            flops=2 * rows * (depth + EXTRA) * count * width,
            bytes_accessed=2 * depth * count * width + 8 * rows * depth,
            transcendentals=0,
        ),
        name="backward_mm",
    )(g, weight, extra, acc, acc_low)


def swiglu_kernel(
    x_ref, lowg_ref, lowu_ref, dy_ref, hlg_ref, g_ref, u_ref, bg_ref, bu_ref, dn_ref, ah_ref,
    second_ref, down_ref, slg_ref, slu_ref, hl_ref, pack_ref,
):
    @pl.when(pl.program_id(0) == 0)
    def _():
        for ref in (second_ref, down_ref, slg_ref, slu_ref, hl_ref):
            ref[...] = jnp.zeros_like(ref)

    gate = linear(x_ref[...], g_ref[...]) + linear(lowg_ref[...], bg_ref[...])
    up = linear(x_ref[...], u_ref[...]) + linear(lowu_ref[...], bu_ref[...])
    back = linear_back(dy_ref[...], dn_ref[...]) + linear(hlg_ref[...], ah_ref[...])
    sig = jax.nn.sigmoid(gate)
    silu = gate * sig
    activated = (silu * up).astype(bf16)
    gate_grad = (back * up * (sig * (1.0 + gate * (1.0 - sig)))).astype(bf16)
    up_grad = (back * silu).astype(bf16)
    down_ref[...] += linear(activated, dn_ref[...])
    hl_ref[...] += linear_back(activated, ah_ref[...])
    second_ref[...] += linear_back(gate_grad, g_ref[...]) + linear_back(up_grad, u_ref[...])
    slg_ref[...] += linear_back(gate_grad, bg_ref[...])
    slu_ref[...] += linear_back(up_grad, bu_ref[...])
    pack_ref[:RANK] = linear_grad(hlg_ref[...], activated).astype(bf16)
    pack_ref[RANK : 2 * RANK] = linear_grad(lowg_ref[...], gate_grad).astype(bf16)
    pack_ref[2 * RANK :] = linear_grad(lowu_ref[...], up_grad).astype(bf16)


def swiglu(x, lowg, lowu, dy, hlg, weight, bg, bu, down, ah):
    rows = x.shape[0]
    width = 512
    steps = FF // width
    whole = lambda v: pl.BlockSpec(v.shape, lambda j: (0,) * v.ndim)
    low = pl.BlockSpec((RANK, width), lambda j: (0, j))
    state = [jax.ShapeDtypeStruct((rows, n), f32) for n in (D, D, RANK, RANK, RANK)]
    return pl.pallas_call(
        swiglu_kernel,
        out_shape=tuple(state) + (jax.ShapeDtypeStruct((3 * RANK, FF), bf16),),
        grid=(steps,),
        in_specs=[whole(v) for v in (x, lowg, lowu, dy, hlg)]
        + [
            pl.BlockSpec((D, width), lambda j: (0, j)),
            pl.BlockSpec((D, width), lambda j: (0, steps + j)),
            low,
            low,
            pl.BlockSpec((width, D), lambda j: (j, 0)),
            low,
        ],
        out_specs=tuple(whole(v) for v in state) + (pl.BlockSpec((3 * RANK, width), lambda j: (0, j)),),
        cost_estimate=pl.CostEstimate(
            flops=12 * rows * D * FF, bytes_accessed=6 * D * FF + 24 * rows * D, transcendentals=rows * FF
        ),
        name="swiglu",
    )(x, lowg, lowu, dy, hlg, weight, weight, bg, bu, down, ah)


MESH = pl.DeviceIdType.MESH


def facts_kernel(facts_ref, forget_ref, facts_all, forget_out, send, recv):
    me, z = lax.axis_index("dp"), lax.axis_index("seq")
    barrier = pltpu.get_barrier_semaphore()
    for m in range(1, 8):
        pl.semaphore_signal(barrier, inc=1, device_id=(me ^ m, z), device_id_type=MESH)
    pl.semaphore_wait(barrier, 7)
    copies = []
    for m in range(1, 8):
        for kind, (src, dst) in enumerate(((facts_ref, facts_all), (forget_ref, forget_out))):
            copies.append(
                pltpu.make_async_remote_copy(
                    src_ref=src,
                    dst_ref=dst.at[me],
                    send_sem=send.at[kind, m],
                    recv_sem=recv.at[kind, m],
                    device_id=(me ^ m, z),
                    device_id_type=MESH,
                )
            )
            copies[-1].start()
    local = [
        pltpu.make_async_copy(facts_ref, facts_all.at[me], send.at[0, 0]),
        pltpu.make_async_copy(forget_ref, forget_out.at[me], send.at[1, 0]),
    ]
    for copy in local:
        copy.start()
    for copy in copies + local:
        copy.wait()


def share_facts(facts, forget):
    vmem = pl.BlockSpec(memory_space=pltpu.VMEM)
    return pl.pallas_call(
        facts_kernel,
        out_shape=(
            jax.ShapeDtypeStruct((8,) + facts.shape, facts.dtype),
            jax.ShapeDtypeStruct((8,) + forget.shape, forget.dtype),
        ),
        in_specs=[vmem, vmem],
        out_specs=(vmem, vmem),
        scratch_shapes=[pltpu.SemaphoreType.DMA((2, 8)), pltpu.SemaphoreType.DMA((2, 8))],
        compiler_params=pltpu.CompilerParams(collective_id=0, has_side_effects=True),
        name="share_facts",
    )(facts, forget)


def remote(src, dst, send, recv, to):
    return pltpu.make_async_remote_copy(
        src_ref=src, dst_ref=dst, send_sem=send, recv_sem=recv, device_id=to, device_id_type=MESH
    )


def peers_of(me, z):
    return [(me ^ m, z) for m in range(1, 8)] + [(me ^ m, z ^ k) for m in (0, 1) for k in (1, 2, 3)]


def greet(me, z):
    barrier = pltpu.get_barrier_semaphore()
    peers = peers_of(me, z)
    for peer in peers:
        pl.semaphore_signal(barrier, inc=1, device_id=peer, device_id_type=MESH)
    pl.semaphore_wait(barrier, len(peers))


class Mover:
    def __init__(self, plan, shards, full, sems):
        self.plan, self.items = plan, []
        self.send, self.recv, self.own = sems
        for (target, first, width, step, shared), src in zip(plan, shards):
            for at in range(0, width, step):
                self.items.append((src, full[target], at, first + at, step, shared))
        self.me, self.z = lax.axis_index("dp"), lax.axis_index("seq")
        core = self.me & 1
        self.odd = self.z & 1
        self.near = self.me ^ (2 + 2 * core)
        self.next = self.me ^ (4 - 2 * core)
        self.far = self.me ^ 6

    def sizes(self, i):
        src, shared = self.items[i][0], self.items[i][5]
        count = src.shape[0]
        return count, shared, count - shared

    def spot(self, i, owner, start, length):
        src, dst, _, first, width, _ = self.items[i]
        rows = pl.ds(pl.multiple_of(owner * src.shape[0] + start, 16), length)
        return dst.at[rows, pl.ds(first, width)]

    def copy(self, i, slot):
        src, dst, at, _, width, _ = self.items[i]
        count, shared, length = self.sizes(i)
        low = self.odd * shared
        cols = pl.ds(at, width)
        owner = {2: self.near, 3: self.near, 4: self.next, 5: self.far, 7: self.near, 8: self.next, 9: self.far,
                 10: self.near, 11: self.next, 12: self.far}
        partner, above = (self.me ^ 1, self.z), (self.me, self.z ^ 1)
        if slot in (0, 1):
            here = src.at[pl.ds(pl.multiple_of(low, 16), length), cols]
            there = self.spot(i, self.me, low, length)
            to = (self.near if slot == 0 else self.next, self.z)
        elif slot == 2:
            here = there = self.spot(i, owner[2], low, length)
            to = (self.next, self.z)
        elif slot in (3, 4, 5):
            here = there = self.spot(i, owner[slot], self.odd * (count - shared), shared)
            to = above
        elif slot == 6:
            here, there, to = src.at[:, cols], self.spot(i, self.me, 0, count), partner
        elif slot in (7, 8, 9):
            here = there = self.spot(i, owner[slot], low, length)
            to = partner
        else:
            here = there = self.spot(i, owner[slot], (1 - self.odd) * (count - shared), shared)
            to = partner
        return remote(here, there, self.send.at[i, slot], self.recv.at[i, slot], to)

    def local(self, i):
        src, _, at, _, width, _ = self.items[i]
        return pltpu.make_async_copy(src.at[:, pl.ds(at, width)], self.spot(i, self.me, 0, src.shape[0]), self.own.at[i])

    def phase(self, i, stage):
        if stage == 0:
            for slot in (0, 1, 6):
                self.copy(i, slot).start()
            self.local(i).start()
        elif stage == 1:
            self.copy(i, 0).wait_recv()
            for slot in (2, 3, 7):
                self.copy(i, slot).start()
            self.copy(i, 1).wait_recv()
            for slot in (4, 8):
                self.copy(i, slot).start()
        elif stage == 2:
            self.copy(i, 2).wait_recv()
            for slot in (5, 9):
                self.copy(i, slot).start()
        else:
            for slot in (3, 4, 5):
                self.copy(i, slot).wait_recv()
                self.copy(i, slot + 7).start()

    def polls(self, count):
        n = len(self.items)
        out = [[] for _ in range(count)]
        out[0] = [(i, 0) for i in range(n)]
        span = max(1, count - 3)
        for stage in (1, 2, 3):
            for i in range(n):
                out[min(count - 1, i * span // n + stage)].append((i, stage))
        return out

    def run(self, poll):
        for i, stage in poll:
            self.phase(i, stage)

    def finish(self):
        for i in range(len(self.items)):
            for slot in range(6, 13):
                self.copy(i, slot).wait_recv()
            for slot in range(13):
                self.copy(i, slot).wait_send()
            self.local(i).wait()


def mover_scratch(plan):
    dma = pltpu.SemaphoreType.DMA
    count = sum(width // step for _, _, width, step, _ in plan)
    return [dma((count, 13)), dma((count, 13)), dma((count,))]


def shard_specs(pieces):
    return [
        pl.BlockSpec((v.shape[0], width), lambda *g, at=at: (0, at), pipeline_mode=pl.Buffered(1))
        for v, at, width in pieces
    ]


def full_shapes(plan, pieces):
    shapes = {}
    for (target, first, width, _, _), (v, _, _) in zip(plan, pieces):
        rows, cols = shapes.get(target, (8 * v.shape[0], 0))
        shapes[target] = (rows, max(cols, first + width))
    return tuple(jax.ShapeDtypeStruct(shapes[t], bf16) for t in sorted(shapes))


def spread_rows(src, dst, send, recv):
    me, z = lax.axis_index("dp"), lax.axis_index("seq")
    core, odd, tree_core = me & 1, z & 1, z >> 1
    for j in range(2):
        for b in range(2):
            to = ((me & ~1) | (b ^ odd), 2 * core + j)
            same = (to[0] == me) & (to[1] == z)
            spot = dst.at[pl.ds(pl.multiple_of(z * BLOCK, BLOCK), BLOCK)]

            @pl.when(same)
            def _():
                pltpu.make_async_copy(src.at[j, b], spot, send.at[2 * j + b]).start()

            @pl.when(jnp.logical_not(same))
            def _():
                remote(src.at[j, b], spot, send.at[2 * j + b], recv.at[z], to).start()


def wait_rows(src, dst, send, recv):
    me, z = lax.axis_index("dp"), lax.axis_index("seq")
    core, odd, tree_core = me & 1, z & 1, z >> 1
    for j in range(2):
        for b in range(2):
            to = ((me & ~1) | (b ^ odd), 2 * core + j)
            same = (to[0] == me) & (to[1] == z)
            spot = dst.at[pl.ds(pl.multiple_of(z * BLOCK, BLOCK), BLOCK)]

            @pl.when(same)
            def _():
                pltpu.make_async_copy(src.at[j, b], spot, send.at[2 * j + b]).wait()

            @pl.when(jnp.logical_not(same))
            def _():
                remote(src.at[j, b], spot, send.at[2 * j + b], recv.at[z], to).wait_send()

    for p in range(4):
        @pl.when(jnp.logical_not((p == z) & (core == tree_core)))
        def _():
            spot = dst.at[pl.ds(p * BLOCK, BLOCK)]
            remote(src.at[0, 0], spot, send.at[p], recv.at[p], (me ^ 1, z)).wait_recv()


def vmem_spec():
    return pl.BlockSpec(memory_space=pltpu.VMEM)


def hbm_spec():
    return pl.BlockSpec(memory_space=pl.ANY)


def full_shape(shard):
    return jax.ShapeDtypeStruct((8 * shard.shape[0], shard.shape[1]), bf16)


FIRST_PLAN = ((1, 0, EXTRA, EXTRA, 48), (0, 0, 4 * D, 512, 48))


def first_kernel(tok, inner, model, ffp, fg, mix, x_o, inner_o, model_o, ff_o, mix_o, fg_o,
                 send, recv, own, small_send, small_recv, row_send, row_recv):
    me, z = lax.axis_index("dp"), lax.axis_index("seq")
    greet(me, z)
    mover = Mover(FIRST_PLAN, (fg, mix), (mix_o, fg_o), (send, recv, own))
    n = len(mover.items)
    for i in range(3):
        mover.phase(i, 0)
    spread_rows(tok, x_o, row_send, row_recv)
    small = []
    for kind, (src, dst) in enumerate(((inner, inner_o), (model, model_o), (ffp, ff_o))):
        for m in range(1, 8):
            small.append(
                remote(src.at[me ^ m], dst.at[me], small_send.at[kind, m], small_recv.at[kind, m], (me ^ m, z))
            )
        small.append(pltpu.make_async_copy(src.at[me], dst.at[me], small_send.at[kind, 0]))
    for copy in small:
        copy.start()
    for t in range(n + 2):
        if t + 3 < n:
            mover.phase(t + 3, 0)
        for stage in (1, 2, 3):
            if 0 <= t - stage + 1 < n:
                mover.phase(t - stage + 1, stage)
    wait_rows(tok, x_o, row_send, row_recv)
    for copy in small:
        copy.wait()
    mover.finish()


def first(tokens, inner, model, ffp, mix, fg):
    args = (tokens.reshape(2, 2, BLOCK, D), inner, model, ffp, fg, mix)
    dma = pltpu.SemaphoreType.DMA
    pieces = ((fg, 0, EXTRA), (mix, 0, 4 * D))
    return pl.pallas_call(
        first_kernel,
        out_shape=(
            jax.ShapeDtypeStruct((4 * BLOCK, D), bf16),
            *(jax.ShapeDtypeStruct(v.shape, bf16) for v in (inner, model, ffp)),
            *full_shapes(FIRST_PLAN, pieces),
        ),
        in_specs=[vmem_spec()] * 6,
        out_specs=(hbm_spec(),) * 6,
        scratch_shapes=mover_scratch(FIRST_PLAN) + [dma((3, 8)), dma((3, 8)), dma((4,)), dma((4,))],
        compiler_params=pltpu.CompilerParams(collective_id=1, has_side_effects=True),
        name="first",
    )(*args)


def lane_groups(shape):
    return lax.broadcasted_iota(jnp.int32, shape, 1) // RANK


def row_groups(shape):
    return lax.broadcasted_iota(jnp.int32, shape, 0) // RANK


def split_refs(plan, refs, outs, extra):
    n = len(plan)
    m = len({target for target, *_ in plan})
    shards, outputs = refs[:n], refs[n : n + outs]
    full, sems, rest = refs[n + outs : n + outs + m], refs[n + outs + m : n + outs + m + 3], refs[n + outs + m + 3 :]
    assert len(rest) == extra
    return shards, outputs, full, sems, rest


def project_kernel(plan, x, gain, inner, got_model, w_ref, w_forget, forget_sel, bias, *refs):
    shards, outputs, full, sems, (csend, crecv) = split_refs(plan, refs, 9, 2)
    norm_o, low_o, kv_o, kv2_o, q_o, gate_o, forget_o, forget2_o, model = outputs
    me, z = lax.axis_index("dp"), lax.axis_index("seq")
    partner = (me ^ 1, z)
    step = pl.program_id(0)
    mover = Mover(plan, shards, full, sems)
    polls = mover.polls(12)
    place = jnp.where(step < 6, step + 3, jnp.where(step < 9, step - 6, step))
    group = place // 3

    def pass_kv(j):
        cols = pl.ds(j * 512, 512)
        return remote(kv_o.at[:, cols], kv2_o.at[:, cols], csend.at[j], crecv.at[j], partner)

    pass_forget = remote(forget_o, forget2_o, csend.at[6], crecv.at[6], partner)

    @pl.when(step == 0)
    def _():
        greet(me, z)
        mover.run(polls[0])
        model[6 * RANK :] = jnp.zeros_like(model[6 * RANK :])
        for d in range(8):
            model[: 6 * RANK, d * 192 : (d + 1) * 192] = got_model[d]
        inputs = x[...].astype(f32)
        norm = (inputs * rms_scale(inputs) * gain[...]).astype(bf16)
        norm_o[...] = norm
        low = linear(norm, inner[...])
        low = jnp.where(lane_groups(low.shape) < 5, low, 0.0).astype(bf16)
        low_o[...] = low
        logit = linear(norm, w_forget[...]) + linear(low, forget_sel[...]) + bias[...]
        forget_o[...] = logit.astype(bf16)

    extra = model[:, pl.ds(pl.multiple_of((place - 3 * group) * 512, 512), 512)]
    extra = jnp.where(row_groups(extra.shape) == group, extra, jnp.zeros_like(extra))
    value = linear(norm_o[...], w_ref[...]) + linear(low_o[...], extra)

    @pl.when(step < 6)
    def _():
        kv_o[:, pl.ds(pl.multiple_of((place - 3) * 512, 512), 512)] = value.astype(bf16)

    @pl.when(group == 0)
    def _():
        q_o[:, pl.ds(pl.multiple_of(place * 512, 512), 512)] = value.astype(bf16)

    @pl.when(group == 3)
    def _():
        gate_o[:, pl.ds(pl.multiple_of((place - 9) * 512, 512), 512)] = value

    for s in range(1, 12):
        @pl.when(step == s)
        def _():
            if s <= 6:
                pass_kv(s - 1).start()
            if s == 1:
                pass_forget.start()
            mover.run(polls[s])
            if s == 11:
                mover.finish()
                pass_forget.wait()
                for j in range(6):
                    pass_kv(j).wait()


def project(x, gain, inner, got_model, w_mix, w_forget, forget_sel, bias, plan, pieces):
    rows = 4 * BLOCK
    block = lambda j: jnp.where(j < 6, j + 3, jnp.where(j < 9, j - 6, j))
    small = lambda v: pl.BlockSpec(v.shape, lambda j: (0,) * v.ndim, pipeline_mode=pl.Buffered(1))
    keep = lambda *shape: pl.BlockSpec(shape, lambda j: (0,) * len(shape))
    dma = pltpu.SemaphoreType.DMA
    sds = jax.ShapeDtypeStruct
    full = full_shapes(plan, pieces)
    return pl.pallas_call(
        functools.partial(project_kernel, plan),
        out_shape=(
            sds((rows, D), bf16), sds((rows, 128), bf16), sds((rows, 2 * D), bf16), sds((rows, 2 * D), bf16),
            sds((rows, D), bf16), sds((rows, D), f32), sds((rows, 128), bf16), sds((rows, 128), bf16),
            sds((128, D), bf16), *full,
        ),
        grid=(12,),
        in_specs=[
            small(x), small(gain), small(inner), small(got_model),
            pl.BlockSpec((D, 512), lambda j: (0, block(j))),
            small(w_forget), small(forget_sel), small(bias),
        ]
        + shard_specs(pieces),
        out_specs=(
            keep(rows, D), keep(rows, 128), keep(rows, 2 * D), hbm_spec(), keep(rows, D), keep(rows, D),
            keep(rows, 128), hbm_spec(), keep(128, D),
        )
        + (hbm_spec(),) * len(full),
        scratch_shapes=mover_scratch(plan) + [dma((7,)), dma((7,))],
        compiler_params=pltpu.CompilerParams(collective_id=3, has_side_effects=True),
        name="project",
    )(x, gain, inner, got_model, w_mix, w_forget, forget_sel, bias, *(v for v, _, _ in pieces))


def paths_kernel_part(forget, forget2, strict, sums):
    row = lax.broadcasted_iota(jnp.int32, (BLOCK, BLOCK), 0)
    col = lax.broadcasted_iota(jnp.int32, (BLOCK, BLOCK), 1)
    lower = (col <= row).astype(f32)
    within, totals = [], []
    for m in range(8):
        ref = forget if m < 4 else forget2
        logit = ref[(m % 4) * BLOCK : (m % 4 + 1) * BLOCK].astype(f32)
        value = jnp.minimum(logit, 0.0) - jnp.log(1.0 + jnp.exp(-jnp.abs(logit)))
        value = jnp.dot(lower, value, precision=highest, preferred_element_type=f32)
        within.append(value)
        totals.append(value[BLOCK - 1 :])
    offsets = jnp.dot(strict[...], jnp.concatenate(totals, axis=0), precision=highest, preferred_element_type=f32)
    for m in range(8):
        sums[m] = -(within[m] + offsets[m : m + 1]).T


UPS = (2, 3, 6, 7)


def key_spots(place, core):
    if place == 0:
        return [4, 0]
    if place == 1:
        return [4 * core, 4 - 4 * core, 5, 1]
    return [4 * core, 4 - 4 * core, 5 - 4 * core, 1 + 4 * core, None, place]


def block_of(m):
    return pl.ds(m * BLOCK if isinstance(m, int) else pl.multiple_of(m * BLOCK, BLOCK), BLOCK)


def key_block(buf, spot, ups, place):
    if spot is not None:
        return buf[block_of(spot), :]
    total = None
    for i, m in enumerate(UPS):
        line = ups[4 * (place - 2) + i : 4 * (place - 2) + i + 1, :].astype(buf.dtype)
        part = buf[block_of(m), :] * line
        total = part if total is None else total + part
    return total


def path_line(sums, spot, head, ups, place):
    if spot is not None:
        return sums[spot, pl.ds(head, 1), :]
    total = None
    for i, m in enumerate(UPS):
        part = sums[m, pl.ds(head, 1), :] * ups[4 * (place - 2) + i : 4 * (place - 2) + i + 1, :]
        total = part if total is None else total + part
    return total


def attend_move_kernel(plan, ups, closed, q_ref, k_ref, v_ref, k2_ref, v2_ref, gate_ref, forget, forget2, strict, cot,
                       *refs):
    shards, outputs, full, sems, rest = split_refs(plan, refs, 4, 5)
    o_ref, gated_ref, p_ref, dy_o = outputs
    kbuf, vbuf, sums, row_send, row_recv = rest
    me, z = lax.axis_index("dp"), lax.axis_index("seq")
    core = me & 1
    step = pl.program_id(0)
    mover = Mover(plan, shards, full, sems)
    polls = mover.polls(PAIRS)

    @pl.when(step == 0)
    def _():
        greet(me, z)
        mover.run(polls[0])
        spread_rows(cot, dy_o, row_send, row_recv)
        paths_kernel_part(forget, forget2, strict, sums)

    half = 4 * BLOCK
    kbuf[:half] = k_ref[...]
    kbuf[half:] = k2_ref[...]
    vbuf[:half] = v_ref[...]
    vbuf[half:] = v2_ref[...]
    lane = lax.broadcasted_iota(jnp.int32, (BLOCK, BLOCK), 1)
    row = lax.broadcasted_iota(jnp.int32, (BLOCK, BLOCK), 0)
    later = jnp.where(lane > row, f32(-1e30), f32(0.0))
    for place in range(4):
        count, first = ENTRIES[place], FIRST[place]
        queries = q_ref[place * BLOCK : (place + 1) * BLOCK, :]
        spots = key_spots(place, core)
        keys = jnp.concatenate([key_block(kbuf, s, ups, place) for s in spots], axis=0)
        values = jnp.concatenate([key_block(vbuf, s, ups, place) for s in spots], axis=0)
        outs = []
        for a in range(2):
            mine = jnp.where((lane < HD) == (a == 0), queries, jnp.zeros_like(queries))
            scores = linear_back(mine, keys) * (HD ** (-0.5))
            bias = [
                path_line(sums, s, 2 * step + a, ups, place) + closed[first + e : first + e + 1, :]
                for e, s in enumerate(spots)
            ]
            scores = scores + jnp.concatenate(bias, axis=1)
            scores = jnp.concatenate(
                [scores[:, : (count - 1) * BLOCK], scores[:, (count - 1) * BLOCK :] + later], axis=1
            )
            peak = jnp.max(scores, axis=1, keepdims=True)
            expo = jnp.exp(scores - peak)
            total = jnp.sum(expo, axis=1, keepdims=True)
            probs = (expo * (1.0 / total)).astype(bf16)
            p_ref[a, :, first * BLOCK : (first + count) * BLOCK] = probs
            outs.append(linear(probs, values))
        span = slice(place * BLOCK, (place + 1) * BLOCK)
        attended = jnp.where(lane < HD, outs[0], outs[1])
        o_ref[span, :] = attended
        gated_ref[span, :] = (attended * jax.nn.sigmoid(gate_ref[span, :])).astype(bf16)

    for s in range(1, PAIRS):
        @pl.when(step == s)
        def _():
            mover.run(polls[s])
            if s == PAIRS - 1:
                mover.finish()
                wait_rows(cot, dy_o, row_send, row_recv)


def attend_move(ups, closed, q, kv, kv2, gate, forget, forget2, strict, cot, plan, pieces):
    rows = pl.BlockSpec((4 * BLOCK, 2 * HD), lambda g: (0, g))
    upper = pl.BlockSpec((4 * BLOCK, 2 * HD), lambda g: (0, PAIRS + g))
    small = lambda v: pl.BlockSpec(v.shape, lambda g: (0,) * v.ndim, pipeline_mode=pl.Buffered(1))
    dma = pltpu.SemaphoreType.DMA
    sds = jax.ShapeDtypeStruct
    cot = cot.reshape(2, 2, BLOCK, D)
    full = full_shapes(plan, pieces)
    return pl.pallas_call(
        functools.partial(attend_move_kernel, plan),
        out_shape=(
            sds((4 * BLOCK, D), f32), sds((4 * BLOCK, D), bf16), sds((H, BLOCK, TOTAL * BLOCK), bf16),
            sds((4 * BLOCK, D), bf16), *full,
        ),
        grid=(PAIRS,),
        in_specs=[small(ups), small(closed), rows, rows, upper, rows, upper, rows]
        + [small(v) for v in (forget, forget2, strict, cot)]
        + shard_specs(pieces),
        out_specs=(rows, rows, pl.BlockSpec((2, BLOCK, TOTAL * BLOCK), lambda g: (g, 0, 0)), hbm_spec())
        + (hbm_spec(),) * len(full),
        scratch_shapes=mover_scratch(plan)
        + [pltpu.VMEM((8 * BLOCK, 2 * HD), bf16)] * 2
        + [pltpu.VMEM((8, BLOCK, BLOCK), f32), dma((4,)), dma((4,))],
        compiler_params=pltpu.CompilerParams(collective_id=4, has_side_effects=True),
        name="attend_move",
    )(ups, closed, q, kv, kv, kv2, kv2, gate, forget, forget2, strict, cot, *(v for v, _, _ in pieces))


def middle_kernel(plan, x, gated, dy, gain, inner, model, w_ref, *refs):
    shards, outputs, full, sems, _ = split_refs(plan, refs, 5, 0)
    mid_o, norm_o, slow_o, plow_o, hlg_o = outputs
    me, z = lax.axis_index("dp"), lax.axis_index("seq")
    step = pl.program_id(0)
    mover = Mover(plan, shards, full, sems)
    polls = mover.polls(6)

    for s in range(3):
        @pl.when(step == s)
        def _():
            if s == 0:
                greet(me, z)
            mover.run(polls[2 * s])

    @pl.when(step == 0)
    def _():
        low = linear(gated[...], inner[...])
        plow_o[...] = jnp.where(lane_groups(low.shape) == 5, low, 0.0).astype(bf16)
        low = linear_back(dy[...], model[...])
        hlg_o[...] = jnp.where(lane_groups(low.shape) == 4, low, 0.0).astype(bf16)

    cols = pl.ds(pl.multiple_of(step * 512, 512), 512)
    mid_o[:, cols] = x[:, cols].astype(f32) + linear(gated[...], w_ref[...]) + linear(plow_o[...], model[:, cols])

    @pl.when(step == 2)
    def _():
        value = mid_o[...]
        norm = (value * rms_scale(value) * gain[...]).astype(bf16)
        norm_o[...] = norm
        low = linear(norm, inner[...])
        slow_o[...] = jnp.where(lane_groups(low.shape) >= 6, low, 0.0).astype(bf16)

    for s in range(3):
        @pl.when(step == s)
        def _():
            mover.run(polls[2 * s + 1])
            if s == 2:
                mover.finish()


def middle_step(x, gated, dy, gain, inner, model, w_out, plan, pieces):
    rows = 4 * BLOCK
    small = lambda v: pl.BlockSpec(v.shape, lambda j: (0,) * v.ndim, pipeline_mode=pl.Buffered(1))
    keep = lambda *shape: pl.BlockSpec(shape, lambda j: (0,) * len(shape))
    sds = jax.ShapeDtypeStruct
    full = full_shapes(plan, pieces)
    return pl.pallas_call(
        functools.partial(middle_kernel, plan),
        out_shape=(
            sds((rows, D), f32), sds((rows, D), bf16), sds((rows, 128), bf16), sds((rows, 128), bf16),
            sds((rows, 128), bf16), *full,
        ),
        grid=(3,),
        in_specs=[small(v) for v in (x, gated, dy, gain, inner, model)]
        + [pl.BlockSpec((D, 512), lambda j: (0, j))]
        + shard_specs(pieces),
        out_specs=(keep(rows, D), keep(rows, D), keep(rows, 128), keep(rows, 128), keep(rows, 128))
        + (hbm_spec(),) * len(full),
        scratch_shapes=mover_scratch(plan),
        compiler_params=pltpu.CompilerParams(collective_id=5, has_side_effects=True),
        name="middle_step",
    )(x, gated, dy, gain, inner, model, w_out, *(v for v, _, _ in pieces))


def feed_kernel(plan, steps, x_ref, slow, dy_ref, hlg, *refs):
    g_ref, u_ref, low, dn_a, dn_b = refs[:5]
    state_in, refs = refs[5:10], refs[10:]
    step = pl.program_id(0)
    if plan:
        shards, outputs, full, sems, _ = split_refs(plan, refs, 6, 0)
        me, z = lax.axis_index("dp"), lax.axis_index("seq")
        mover = Mover(plan, shards, full, sems)
        polls = mover.polls(3 * steps)
    else:
        outputs = refs
    state, pack_ref = outputs[:5], outputs[5]
    second_ref, down_ref, slg_ref, slu_ref, hl_ref = state

    def poll(part):
        if plan:
            for s in range(steps):
                @pl.when(step == s)
                def _():
                    if s == 0 and part == 0:
                        greet(me, z)
                    mover.run(polls[3 * s + part])
                    if s == steps - 1 and part == 2:
                        mover.finish()

    poll(0)

    @pl.when(step == 0)
    def _():
        for ref, old in zip(state, state_in):
            ref[...] = old[...]

    lowg, lowu, hidden = slow[:, 6 * RANK : 7 * RANK], slow[:, 7 * RANK :], hlg[:, 4 * RANK : 5 * RANK]
    ah, bg, bu = low[:RANK], low[RANK : 2 * RANK], low[2 * RANK :]
    edge = dn_a.shape[1]
    gate = linear(x_ref[...], g_ref[...]) + linear(lowg, bg)
    up = linear(x_ref[...], u_ref[...]) + linear(lowu, bu)
    back = linear_back(dy_ref[:, :edge], dn_a[...]) + linear_back(dy_ref[:, edge:], dn_b[...]) + linear(hidden, ah)
    poll(1)
    sig = jax.nn.sigmoid(gate)
    silu = gate * sig
    activated = (silu * up).astype(bf16)
    gate_grad = (back * up * (sig * (1.0 + gate * (1.0 - sig)))).astype(bf16)
    up_grad = (back * silu).astype(bf16)
    down_ref[:, :edge] += linear(activated, dn_a[...])
    down_ref[:, edge:] += linear(activated, dn_b[...])
    hl_ref[...] += linear_back(activated, ah)
    second_ref[...] += linear_back(gate_grad, g_ref[...]) + linear_back(up_grad, u_ref[...])
    slg_ref[...] += linear_back(gate_grad, bg)
    slu_ref[...] += linear_back(up_grad, bu)
    pack_ref[:RANK] = linear_grad(hidden, activated).astype(bf16)
    pack_ref[RANK : 2 * RANK] = linear_grad(lowg, gate_grad).astype(bf16)
    pack_ref[2 * RANK :] = linear_grad(lowu, up_grad).astype(bf16)
    poll(2)


def feed(x, slow, dy, hlg, weight, low, downs, chunk, state, plan, pieces, ident):
    rows = 4 * BLOCK
    steps, width = 2, 512
    small = lambda v: pl.BlockSpec(v.shape, lambda j: (0,) * v.ndim, pipeline_mode=pl.Buffered(1))
    keep = lambda v: pl.BlockSpec(v.shape, lambda j: (0,) * v.ndim)
    owned = pl.BlockSpec((None, 3 * RANK, width), lambda j: (2 * chunk + j, 0, 0))
    down = lambda v: pl.BlockSpec((width, v.shape[1]), lambda j: (2 * chunk + j, 0))
    params = {}
    if plan:
        params["compiler_params"] = pltpu.CompilerParams(collective_id=ident, has_side_effects=True)
    full = full_shapes(plan, pieces)
    return pl.pallas_call(
        functools.partial(feed_kernel, plan, steps),
        out_shape=tuple(jax.ShapeDtypeStruct(v.shape, v.dtype) for v in state)
        + (jax.ShapeDtypeStruct((steps, 3 * RANK, width), bf16),)
        + full,
        grid=(steps,),
        in_specs=[small(v) for v in (x, slow, dy, hlg)]
        + [
            pl.BlockSpec((D, width), lambda j: (0, j)),
            pl.BlockSpec((D, width), lambda j: (0, 2 + j)),
            owned,
            down(downs[0]),
            down(downs[1]),
        ]
        + [small(v) for v in state]
        + shard_specs(pieces),
        out_specs=tuple(keep(v) for v in state)
        + (pl.BlockSpec((None, 3 * RANK, width), lambda j: (j, 0, 0)),)
        + (hbm_spec(),) * len(full),
        scratch_shapes=mover_scratch(plan) if plan else [],
        name="feed",
        **params,
    )(x, slow, dy, hlg, weight, weight, low, *downs, *state, *(v for v, _, _ in pieces))


def attend_return_kernel(
    ups, q_ref, k_ref, v_ref, k2_ref, v2_ref, g_ref, o_ref, p_ref,
    dq_ref, dk_ref, dv_ref, qsum_ref, ksum_ref, kbuf, vbuf, dkbuf, dvbuf,
):
    core = lax.axis_index("dp") & 1
    half = 4 * BLOCK
    pair = pl.program_id(0)
    kbuf[:half] = k_ref[...]
    kbuf[half:] = k2_ref[...]
    vbuf[:half] = v_ref[...]
    vbuf[half:] = v2_ref[...]
    dkbuf[...] = jnp.zeros_like(dkbuf)
    dvbuf[...] = jnp.zeros_like(dvbuf)

    @pl.when(pair == 0)
    def _():
        qsum_ref[...] = jnp.zeros_like(qsum_ref)
        ksum_ref[...] = jnp.zeros_like(ksum_ref)

    lane = lax.broadcasted_iota(jnp.int32, (BLOCK, BLOCK), 1)
    scale = HD ** (-0.5)
    for place in range(4):
        count, first = ENTRIES[place], FIRST[place]
        span = slice(place * BLOCK, (place + 1) * BLOCK)
        queries = q_ref[span, :]
        grads = g_ref[span, :]
        product = grads.astype(f32) * o_ref[span, :]
        spots = key_spots(place, core)
        keys = jnp.concatenate([key_block(kbuf, s, ups, place) for s in spots], axis=0)
        values = jnp.concatenate([key_block(vbuf, s, ups, place) for s in spots], axis=0)
        dqs, dks, dvs = [], [], []
        row_sums = qsum_ref[span, :]
        for a in range(2):
            own = (lane < HD) == (a == 0)
            dot_row = jnp.sum(jnp.where(own, product, 0.0), axis=1, keepdims=True)
            mine = jnp.where(own, grads, jnp.zeros_like(grads))
            probs = p_ref[a, :, first * BLOCK : (first + count) * BLOCK]
            prob_grad = linear_back(mine, values)
            score_grad = (probs.astype(f32) * (prob_grad - dot_row)).astype(bf16)
            wide = score_grad.astype(f32)
            col = jnp.sum(wide, axis=0, keepdims=True)
            head = pl.ds(2 * pair + a, 1)
            for e, spot in enumerate(spots):
                part = col[:, e * BLOCK : (e + 1) * BLOCK]
                if spot is not None:
                    ksum_ref[spot, head, :] += part
                else:
                    for i, m in enumerate(UPS):
                        ksum_ref[m, head, :] += part * ups[4 * (place - 2) + i : 4 * (place - 2) + i + 1, :]
            row_sums = row_sums + jnp.where(lane == 2 * pair + a, jnp.sum(wide, axis=1, keepdims=True), 0.0)
            dqs.append(linear(score_grad, keys))
            dks.append(linear_grad(score_grad, queries))
            dvs.append(linear_grad(probs, grads))
        qsum_ref[span, :] = row_sums
        dq_ref[span, :] = (jnp.where(lane < HD, dqs[0], dqs[1]) * scale).astype(bf16)
        for e, spot in enumerate(spots):
            part = slice(e * BLOCK, (e + 1) * BLOCK)
            dk_part = jnp.where(lane < HD, dks[0][part], dks[1][part])
            dv_part = jnp.where(lane < HD, dvs[0][part], dvs[1][part])
            if spot is not None:
                dkbuf[block_of(spot), :] += dk_part
                dvbuf[block_of(spot), :] += dv_part
            else:
                for i, m in enumerate(UPS):
                    line = ups[4 * (place - 2) + i : 4 * (place - 2) + i + 1, :]
                    dkbuf[block_of(m), :] += dk_part * line
                    dvbuf[block_of(m), :] += dv_part * line
    dk_ref[...] = (dkbuf[...] * scale).astype(bf16)
    dv_ref[...] = dvbuf[...].astype(bf16)


def attend_return(ups, queries, kv, kv2, grads, attended, probs):
    rows = pl.BlockSpec((4 * BLOCK, 2 * HD), lambda g: (0, g))
    upper = pl.BlockSpec((4 * BLOCK, 2 * HD), lambda g: (0, PAIRS + g))
    full = pl.BlockSpec((8 * BLOCK, 2 * HD), lambda g: (0, g))
    sds = jax.ShapeDtypeStruct
    return pl.pallas_call(
        attend_return_kernel,
        out_shape=(
            sds((4 * BLOCK, D), bf16), sds((8 * BLOCK, D), bf16), sds((8 * BLOCK, D), bf16),
            sds((4 * BLOCK, BLOCK), f32), sds((8, BLOCK, BLOCK), f32),
        ),
        grid=(PAIRS,),
        in_specs=[
            pl.BlockSpec(ups.shape, lambda g: (0, 0)), rows, rows, upper, rows, upper, rows, rows,
            pl.BlockSpec((2, BLOCK, TOTAL * BLOCK), lambda g: (g, 0, 0)),
        ],
        out_specs=(
            rows, full, full, pl.BlockSpec((4 * BLOCK, BLOCK), lambda g: (0, 0)),
            pl.BlockSpec((8, BLOCK, BLOCK), lambda g: (0, 0, 0)),
        ),
        scratch_shapes=[pltpu.VMEM((8 * BLOCK, 2 * HD), bf16)] * 2 + [pltpu.VMEM((8 * BLOCK, 2 * HD), f32)] * 2,
        cost_estimate=pl.CostEstimate(flops=16_000_000_000, bytes_accessed=35_000_000, transcendentals=0),
        name="attend_return",
    )(ups, queries, kv, kv, kv2, kv2, grads, attended, probs)


def turn_kernel(
    qsum, ksum, logit, strict, dq, dg, dk, dv, dk2, dv2, w_ref, e_ref, low_ref, a_in, w_forget, forget_sel,
    x_ref, gain, mgrad, ff, early,
    dx_home, ff_trees, early_trees, late_trees,
    grads, acc, lows, path, path2, got_k, got_v, dx, pack, late, ff_got, early_got, late_got,
    ff_sum, early_sum, late_sum, csend, crecv, asend, arecv, zsend, zrecv, xsend, xrecv,
):
    me, z = lax.axis_index("dp"), lax.axis_index("seq")
    core, odd, tree_core = me & 1, z & 1, z >> 1
    step = pl.program_id(0)
    rows = 4 * BLOCK
    partner = (me ^ 1, z)

    swaps = [
        remote(src, dst, csend.at[i], crecv.at[i], partner)
        for i, (src, dst) in enumerate(((path, path2), (dk2, got_k), (dv2, got_v)))
    ]
    packs = ((ff, ff_got, ff_sum, ff_trees), (early, early_got, early_sum, early_trees), (late, late_got, late_sum, late_trees))

    def owners(kind):
        src, dst = packs[kind][:2]
        return [
            remote(src.at[me ^ m], dst.at[me], asend.at[kind, m], arecv.at[kind, m], (me ^ m, z)) for m in range(1, 8)
        ]

    def planes(kind):
        src, dst = packs[kind][2:]
        return [remote(src, dst.at[k], zsend.at[kind, k], zrecv.at[kind, k], (me, z ^ k)) for k in (1, 2, 3)]

    def own_copy(kind):
        src, dst = packs[kind][2:]
        return pltpu.make_async_copy(src, dst.at[0], zsend.at[kind, 0])

    def send_to_owners(kind):
        for copy in owners(kind):
            copy.start()

    def sum_and_send(kind):
        src, got, total = packs[kind][:3]
        got[me] = src[me]
        for copy in owners(kind):
            copy.wait()
        for q in range(4):
            total[q] = (got[2 * q].astype(f32) + got[2 * q + 1].astype(f32)).astype(bf16)
        for copy in planes(kind) + [own_copy(kind)]:
            copy.start()

    lane = lax.broadcasted_iota(jnp.int32, (rows, 128), 1)
    low16 = lambda value, source, target: jnp.where(
        lane // RANK == target, pltpu.roll(value, (target - source) * RANK % 128, 1), jnp.zeros_like(value)
    )

    @pl.when(step == 0)
    def _():
        greet(me, z)
        swaps[1].start()
        swaps[2].start()
        send_to_owners(0)
        send_to_owners(1)
        for m in range(8):
            sums = ksum[m].T
            part = slice(m * BLOCK, (m + 1) * BLOCK)
            path[part] = qsum[part] - sums if m < 4 else -sums
        swaps[0].start()
        grads[:, :D] = dq[...]
        grads[:, 3 * D :] = dg[...]
        acc[...] = jnp.zeros_like(acc)
        lows[...] = jnp.zeros_like(lows)
        pack[...] = jnp.zeros_like(pack)

    @pl.when(step == 3)
    def _():
        sum_and_send(0)

    @pl.when(step == 4)
    def _():
        sum_and_send(1)

    @pl.when(step == 6)
    def _():
        swaps[1].wait()
        swaps[2].wait()
        grads[:, D : 2 * D] = (dk[...].astype(f32) + got_k[...].astype(f32)).astype(bf16)
        grads[:, 2 * D : 3 * D] = (dv[...].astype(f32) + got_v[...].astype(f32)).astype(bf16)

    place = jnp.where(step < 3, step, jnp.where(step < 6, step + 6, step - 3))
    now = grads[:, pl.ds(pl.multiple_of(place * 512, 512), 512)]
    acc[...] += linear_back(now, w_ref[...])
    group = place // 3
    extra = e_ref[...]
    lows[...] += linear_back(now, jnp.where(row_groups(extra.shape) == group, extra, jnp.zeros_like(extra)))
    low = low_ref[...]
    moved = jnp.where(
        group == 0, low16(low, 0, 4), jnp.where(group == 1, low16(low, 1, 5), low16(low, 2, 6))
    )

    @pl.when(group < 3)
    def _():
        spot = pl.ds(pl.multiple_of((place - 3 * group) * 512, 512), 512)
        pack[spot, :] += linear_grad(now, moved)

    @pl.when(step == 11)
    def _():
        swaps[0].wait()
        row = lax.broadcasted_iota(jnp.int32, (BLOCK, BLOCK), 0)
        col = lax.broadcasted_iota(jnp.int32, (BLOCK, BLOCK), 1)
        upper = (row <= col).astype(f32)
        totals = []
        full = []
        for m in range(8):
            theirs = (m + 4) % 8
            value = path[m * BLOCK : (m + 1) * BLOCK] + path2[theirs * BLOCK : (theirs + 1) * BLOCK]
            full.append(value)
            totals.append(jnp.sum(value, axis=0, keepdims=True))
        below = lax.dot_general(
            strict[...], jnp.concatenate(totals, axis=0), (((0,), (0,)), ((), ())), precision=highest,
            preferred_element_type=f32,
        )
        suffix = jnp.concatenate(
            [jnp.dot(upper, full[m], precision=highest, preferred_element_type=f32) + below[m : m + 1] for m in range(4)],
            axis=0,
        )
        forget_low = (suffix * jax.nn.sigmoid(-logit[...].astype(f32))).astype(bf16)
        inner_f = linear_back(forget_low, forget_sel[...])
        ilg = jnp.where(lane < 4 * RANK, lows[...], pltpu.roll(inner_f, 4 * RANK, 1)).astype(bf16)
        first_grad = acc[...] + linear_back(ilg, a_in[...]) + linear_back(forget_low, w_forget[...])
        inputs = x_ref[...].astype(f32)
        scale_rows = rms_scale(inputs)
        unit = inputs * scale_rows
        up = first_grad * gain[...]
        back = scale_rows * (up - unit * jnp.mean(up * unit, axis=-1, keepdims=True))
        dx[...] = (mgrad[...] + back).astype(bf16)
        sends = []
        for p in range(4):
            to = ((me & ~1) | tree_core, p)
            b = core ^ (p & 1)
            self_copy = (to[0] == me) & (p == z)
            src = dx.at[pl.ds(p * BLOCK, BLOCK)]
            dst = dx_home.at[odd, b]
            far = remote(src, dst, xsend.at[p], xrecv.at[2 * odd + b], to)
            near = pltpu.make_async_copy(src, dst, xsend.at[p])
            sends.append((self_copy, near, far))
        first_norm = (unit * gain[...]).astype(bf16)
        keep = jnp.where(lane < 3 * RANK, ilg, low16(ilg, 4, 3))
        body = pack[...] + linear_grad(first_norm, keep)
        forget_piece = linear_grad(forget_low, low16(low_ref[...], 4, 7))
        for d in range(8):
            part = body[d * 192 : (d + 1) * 192]
            late[d] = part.astype(bf16)
            late[d, :32] = (part[:32] + forget_piece[:32]).astype(bf16)
        for self_copy, near, far in sends:
            @pl.when(self_copy)
            def _(near=near):
                near.start()

            @pl.when(jnp.logical_not(self_copy))
            def _(far=far):
                far.start()

        send_to_owners(2)
        sum_and_send(2)
        for kind in range(3):
            own_copy(kind).wait()
            for copy in planes(kind):
                copy.wait()
        for self_copy, near, far in sends:
            @pl.when(self_copy)
            def _(near=near):
                near.wait()

            @pl.when(jnp.logical_not(self_copy))
            def _(far=far):
                far.wait_send()

        for j in range(2):
            for b in range(2):
                from_me = ((b ^ odd) == core) & (2 * core + j == z)
                arrived = remote(
                    dx.at[pl.ds(0, BLOCK)], dx_home.at[j, b], xsend.at[2 * j + b], xrecv.at[2 * j + b], partner
                )

                @pl.when(jnp.logical_not(from_me))
                def _(arrived=arrived):
                    arrived.wait_recv()


def turn(qsum, ksum, logit, strict, dq, dg, dk_all, dv_all, weight, extra, low, a_in, w_forget, forget_sel, x, gain, mgrad, ff, early):
    rows = 4 * BLOCK
    block = lambda j: jnp.where(j < 3, j, jnp.where(j < 6, j + 6, j - 3))
    one = lambda v: pl.BlockSpec(v.shape, lambda j: (0,) * v.ndim, pipeline_mode=pl.Buffered(1))
    top = pl.BlockSpec((rows, D), lambda j: (0, 0), pipeline_mode=pl.Buffered(1))
    bottom = pl.BlockSpec((rows, D), lambda j: (1, 0), pipeline_mode=pl.Buffered(1))
    hbm = pl.BlockSpec(memory_space=pl.ANY)
    dma = pltpu.SemaphoreType.DMA
    vm = pltpu.VMEM
    trees = lambda v: (4,) + v.shape[1:]
    late_shape = (8, D // 8, 128)
    return pl.pallas_call(
        turn_kernel,
        out_shape=(
            jax.ShapeDtypeStruct((2, 2, BLOCK, D), bf16),
            jax.ShapeDtypeStruct((4,) + trees(ff), bf16),
            jax.ShapeDtypeStruct((4,) + trees(early), bf16),
            jax.ShapeDtypeStruct((4, 4) + late_shape[1:], bf16),
        ),
        grid=(12,),
        in_specs=[one(v) for v in (qsum, ksum, logit, strict, dq, dg)]
        + [top, top, bottom, bottom]
        + [
            pl.BlockSpec((D, 512), lambda j: (0, block(j))),
            pl.BlockSpec((128, 512), lambda j: (0, j % 3)),
        ]
        + [one(v) for v in (low, a_in, w_forget, forget_sel, x, gain, mgrad, ff, early)],
        out_specs=(hbm,) * 4,
        scratch_shapes=[
            vm((rows, 4 * D), bf16),
            vm((rows, D), f32),
            vm((rows, 128), f32),
            vm((2 * rows, 128), f32),
            vm((2 * rows, 128), f32),
            vm((rows, D), bf16),
            vm((rows, D), bf16),
            vm((rows, D), bf16),
            vm((D, 128), f32),
            vm(late_shape, bf16),
            vm(ff.shape, bf16),
            vm(early.shape, bf16),
            vm(late_shape, bf16),
            vm(trees(ff), bf16),
            vm(trees(early), bf16),
            vm((4,) + late_shape[1:], bf16),
            dma((3,)),
            dma((3,)),
            dma((3, 8)),
            dma((3, 8)),
            dma((3, 4)),
            dma((3, 4)),
            dma((4,)),
            dma((4,)),
        ],
        compiler_params=pltpu.CompilerParams(collective_id=2, has_side_effects=True),
        name="turn",
    )(
        qsum, ksum, logit, strict, dq, dg, dk_all, dv_all, dk_all, dv_all, weight, extra, low, a_in, w_forget,
        forget_sel, x, gain, mgrad, ff, early,
    )


def body_paired(
    tokens,
    cotangent,
    parents,
    adapter_ids,
    attention_gain,
    mixer_weight,
    forget_weight,
    forget_bias,
    output_weight,
    feedforward_gain,
    swiglu_weight,
    down_weight,
    adapter_inner,
    adapter_hidden,
    adapter_model,
    adapter_project,
    adapter_swiglu,
    adapter_forget,
):
    dp = 8
    me = lax.axis_index("dp")
    z = lax.axis_index("seq")
    core = me & 1
    tree_core, tree_slot = z >> 1, z & 1
    rows = 4 * BLOCK
    wide, tall = D // dp, FF // dp
    part = tall // 4

    def collect(value):
        cut = value.reshape(4, BLOCK, D)
        got = []
        for step in range(4):
            high, low = step >> 1, step & 1
            pairs = []
            for d in range(dp):
                for s in range(4):
                    target = ((d & ~1) | (low ^ (s & 1))) * 4 + 2 * (d & 1) + (high ^ (s >> 1))
                    pairs.append((target, d * 4 + s))
            piece = lax.dynamic_index_in_dim(cut, step ^ (2 * tree_slot + core), 0, keepdims=False)
            got.append(lax.ppermute(piece, ("dp", "seq"), pairs))
        stacked = jnp.stack(got).reshape(2, 2 * BLOCK, D)
        return jnp.stack([lax.dynamic_index_in_dim(stacked, t ^ (z >> 1), 0, keepdims=False) for t in range(2)])

    facts = jnp.concatenate([parents, adapter_ids[:, None]], axis=1)
    facts, forget_all = share_facts(
        jnp.pad(facts, ((0, 6), (0, 128 - 9))), jnp.pad(adapter_forget, ((0, 0), (0, EXTRA - H)))
    )
    facts = facts[:, :2, :9].reshape(2 * dp, 9)
    all_ids = facts[:, 8]
    tree = 2 * ((me & ~1) | tree_core) + tree_slot
    parent_row = lax.dynamic_index_in_dim(facts, tree, 0, keepdims=False)[:8]
    which = lax.dynamic_index_in_dim(all_ids, tree, 0, keepdims=False)
    forget_sel = lax.dynamic_index_in_dim(forget_all, which, 0, keepdims=False)

    def to_trees(value):
        sent = []
        for d in range(dp):
            chosen = lax.dynamic_index_in_dim(
                all_ids, 2 * ((d & ~1) | tree_core) + tree_slot, 0, keepdims=False
            )
            sent.append(lax.dynamic_index_in_dim(value, chosen, 0, keepdims=False))
        return jnp.stack(sent)

    own_inner = to_trees(adapter_inner)
    own_model = to_trees(jnp.concatenate([adapter_model, adapter_project], axis=1))
    own_ff = to_trees(jnp.concatenate([jnp.swapaxes(adapter_hidden, 1, 2), adapter_swiglu], axis=1))
    padded_forget = jnp.pad(forget_weight, ((0, 0), (0, EXTRA - H)))
    x, got_inner, got_model, got_ff, w_mix, w_forget = first(
        tokens, own_inner, own_model, own_ff, mixer_weight, padded_forget
    )
    inner_sel = got_inner.reshape(D, 8 * RANK)
    forget_low = jnp.pad(forget_sel, ((4 * RANK, 128 - 5 * RANK), (0, 0)))
    forget_top = jnp.pad(forget_sel, ((0, 128 - RANK), (0, 0)))
    bias = jnp.pad(forget_bias, (0, EXTRA - H))[None]
    halves = lambda j: ((swiglu_weight, j, 1024), (swiglu_weight, 4 + j, 1024))

    first_norm, low, kv, kv2, queries, gate_logit, forget, forget2, model_sel, w_out, down_a = project(
        x, attention_gain[None], inner_sel, got_model, w_mix, w_forget, forget_low, bias,
        ((0, 0, D, 512, 64), (1, 0, 512, 512, 176)), ((output_weight, 0, D), (down_weight, 0, 512)),
    )

    table = jnp.array([[0, 3, 4, 7], [1, 2, 5, 6]], dtype=jnp.int32)
    ids = jnp.where(core == 0, table.reshape(8), table[::-1].reshape(8))
    parent_of = jnp.sum(jnp.where(ids[:, None] == jnp.arange(8)[None, :], parent_row[None, :], 0), axis=1)
    a, b = ids[:, None], ids[None, :]
    linked = (a >= 4) & (b >= 4) & (parent_of[:, None] == b)
    strict_local = (((b < 4) & (b < a)) | linked).astype(f32)
    up = jnp.concatenate([linked[2, 2:4], linked[2, 6:8], linked[3, 2:4], linked[3, 6:8]]).astype(f32)
    ups = jnp.broadcast_to(up[:, None], (8, BLOCK))
    entry = jnp.arange(24)
    no_up = jnp.where(entry < 12, jnp.sum(up[:4]), jnp.sum(up[4:])) < 0.5
    shut = (
        ((entry == 0) & (core == 0)) | ((entry == 4) & (core == 1)) | (((entry == 10) | (entry == 16)) & no_up)
    )
    closed = jnp.broadcast_to(jnp.where(shut, -1e30, 0.0).astype(f32)[:, None], (24, BLOCK))

    attended, gated, probs, dy, down_b, w_sw0 = attend_move(
        ups, closed, queries, kv, kv2, gate_logit, forget, forget2, strict_local, cotangent,
        ((0, 0, 512, 512, 64), (0, 512, 512, 512, 64), (1, 0, 1024, 512, 32), (1, 1024, 1024, 512, 32)),
        ((down_weight, 1, 512), (down_weight, 2, 512)) + halves(0),
    )
    both = ((0, 0, 1024, 512, 64), (0, 1024, 1024, 512, 64))
    middle, second_norm, slow, plow, hlg, w_sw1 = middle_step(
        x, gated, dy, feedforward_gain[None], inner_sel, model_sel, w_out, both, halves(1)
    )
    zeros = lambda n: jnp.zeros((rows, n), f32)
    state = (zeros(D), zeros(D), zeros(RANK), zeros(RANK), zeros(RANK))
    go = lambda w, j, st, plan, pieces, ident: feed(
        second_norm, slow, dy, hlg, w, got_ff, (down_a, down_b), j, st, plan, pieces, ident
    )
    *state, pack0, w_sw2 = go(w_sw0, 0, state, both, halves(2), 6)
    *state, pack1, w_sw3 = go(w_sw1, 1, state, both, halves(3), 7)
    *state, pack2 = go(w_sw2, 2, state, (), (), None)
    *state, pack3 = go(w_sw3, 3, state, (), (), None)
    second_out, down_out, slg, slu, hidden_low = state

    a_in = jnp.where(jnp.arange(128)[None, :] < 5 * RANK, inner_sel, 0).astype(bf16)
    a_project = inner_sel[:, 5 * RANK : 6 * RANK]
    a_swiglu = inner_sel[:, 6 * RANK :]
    b_g, b_down, b_project = (model_sel[i * RANK : (i + 1) * RANK] for i in (3, 4, 5))
    hidden_low = hidden_low.astype(bf16)
    result = (middle + down_out + linear(hidden_low, b_down)).astype(bf16)

    swiglu_low_grad = jnp.concatenate([slg, slu], axis=1).astype(bf16)
    second_grad = second_out + linear_back(swiglu_low_grad, a_swiglu)
    middle_grad = dy.astype(f32) + norm_back(middle, feedforward_gain, second_grad)
    branch_grad = middle_grad.astype(bf16)
    project_low_grad = linear_back(branch_grad, b_project).astype(bf16)
    gated_grad = backward_mm(
        branch_grad, w_out, jnp.zeros((EXTRA, D), bf16), 0, 3, 512, linear_back(project_low_grad, a_project), zeros(EXTRA)
    )[0]
    gate_open = jax.nn.sigmoid(gate_logit)
    attended_grad = (gated_grad * gate_open).astype(bf16)
    gate_logit_grad = (gated_grad * attended * gate_open * (1.0 - gate_open)).astype(bf16)

    attended_grad, result = lax.optimization_barrier((attended_grad, result))
    outputs = collect(result)
    dq, dk_all, dv_all, query_sum, key_sum = attend_return(
        ups, queries, kv, kv2, attended_grad, attended, probs
    )
    inner_g_grad = linear_back(gate_logit_grad, b_g).astype(bf16)
    early = jnp.concatenate(
        [
            linear_grad(gated, project_low_grad),
            linear_grad(second_norm, swiglu_low_grad),
            linear_grad(first_norm, inner_g_grad),
            linear_grad(dy, hidden_low),
            linear_grad(branch_grad, plow[:, 5 * RANK : 6 * RANK]),
            linear_grad(gate_logit_grad, low[:, 3 * RANK : 4 * RANK]),
            jnp.zeros((D, RANK), f32),
        ],
        axis=1,
    ).astype(bf16).reshape(dp, wide, 128)
    ff_pack = jnp.concatenate([pack0, pack1, pack2, pack3], axis=0)
    early, outputs = lax.optimization_barrier((early, outputs))
    dx, ff_trees, early_trees, late_trees = turn(
        query_sum, key_sum, forget, strict_local, dq, gate_logit_grad, dk_all, dv_all,
        w_mix, model_sel, low, a_in, w_forget, forget_top, x, attention_gain[None], middle_grad, ff_pack, early,
    )
    input_grads = dx.reshape(2, 2 * BLOCK, D).astype(f32)
    ff_trees, early_trees, late_trees = (
        v.reshape((16,) + v.shape[2:]) for v in (ff_trees, early_trees, late_trees)
    )

    chip = jnp.arange(dp // 2, dtype=jnp.int32)
    at = jnp.arange(4, dtype=jnp.int32) ^ z
    tree_of = 2 * (2 * chip[None, :] + (at >> 1)[:, None]) + (at & 1)[:, None]
    id_of = all_ids[tree_of.reshape(-1)]
    one_hot = (jnp.arange(ADAPTERS, dtype=jnp.int32)[:, None] == id_of[None, :]).astype(bf16)

    def by_adapter(value):
        return jnp.einsum("at,trc->arc", one_hot, value, preferred_element_type=f32)

    ff_sum, early_sum, late_sum = by_adapter(ff_trees), by_adapter(early_trees), by_adapter(late_trees)
    turned = lambda v: jnp.swapaxes(v, 1, 2)
    at16 = lambda v, i, n=1: v[:, :, i * RANK : (i + n) * RANK]
    per = ADAPTERS * RANK // dp
    forget_sum = turned(at16(late_sum, 7)[:, :H]).reshape(ADAPTERS * RANK, H)
    return (
        outputs,
        input_grads,
        jnp.concatenate(
            [at16(late_sum, 0, 3), at16(early_sum, 3), at16(late_sum, 3), at16(early_sum, 0, 3)], axis=2
        ),
        turned(ff_sum[:, :RANK]),
        turned(jnp.concatenate([at16(late_sum, 4, 3), at16(early_sum, 6), at16(early_sum, 4)], axis=2)),
        turned(at16(early_sum, 5)),
        ff_sum[:, RANK:],
        lax.dynamic_slice_in_dim(forget_sum, me * per, per, 0),
    )


def body_plain(
    devices,
    tokens,
    cotangent,
    parents,
    adapter_ids,
    attention_gain,
    mixer_weight,
    forget_weight,
    forget_bias,
    output_weight,
    feedforward_gain,
    swiglu_weight,
    down_weight,
    adapter_inner,
    adapter_hidden,
    adapter_model,
    adapter_project,
    adapter_swiglu,
    adapter_forget,
):
    dp, seq = devices
    me = lax.axis_index("dp")
    z = lax.axis_index("seq")
    core = me & 1
    tree_core, tree_slot = z >> 1, z & 1
    rows = 4 * BLOCK
    wide = D // dp
    tall = FF // dp

    def swap(value, bit):
        return lax.ppermute(value, "dp", [(i, i ^ bit) for i in range(dp)])

    def routes(step):
        high, low = step >> 1, step & 1
        pairs = []
        for d in range(dp):
            for s in range(seq):
                slot = high ^ (s >> 1)
                target = ((d & ~1) | (low ^ (s & 1))) * seq + 2 * (d & 1) + slot
                pairs.append((d * seq + s, target))
        return pairs

    def spread(value):
        cut = value.reshape(2, 2, BLOCK, D)
        got = []
        for step in range(4):
            piece = lax.dynamic_index_in_dim(cut[:, step & 1], (step >> 1) ^ (z >> 1), 0, keepdims=False)
            got.append(lax.ppermute(piece, ("dp", "seq"), routes(step)))
        stacked = jnp.stack(got)
        order = [lax.dynamic_index_in_dim(stacked, p ^ (2 * tree_slot + core), 0, keepdims=False) for p in range(4)]
        return jnp.concatenate(order, axis=0)

    def collect(value):
        cut = value.reshape(4, BLOCK, D)
        got = []
        for step in range(4):
            piece = lax.dynamic_index_in_dim(cut, step ^ (2 * tree_slot + core), 0, keepdims=False)
            got.append(lax.ppermute(piece, ("dp", "seq"), [(b, a) for a, b in routes(step)]))
        stacked = jnp.stack(got).reshape(2, 2 * BLOCK, D)
        order = [lax.dynamic_index_in_dim(stacked, t ^ (z >> 1), 0, keepdims=False) for t in range(2)]
        return jnp.stack(order)

    def gather_small(value):
        bit = 1
        while bit < dp:
            other = swap(value, bit)
            flag = (me & bit) != 0
            value = jnp.concatenate([jnp.where(flag, other, value), jnp.where(flag, value, other)], axis=0)
            bit *= 2
        return value

    facts = jnp.concatenate([parents, adapter_ids[:, None]], axis=1)
    facts = gather_small(facts)
    forget_all = gather_small(adapter_forget)
    all_ids = facts[:, 8]
    tree = 2 * ((me & ~1) | tree_core) + tree_slot
    parent_row = lax.dynamic_index_in_dim(facts, tree, 0, keepdims=False)[:8]
    which = lax.dynamic_index_in_dim(all_ids, tree, 0, keepdims=False)

    def to_trees(value):
        sent = []
        for d in range(dp):
            owner_tree = 2 * ((d & ~1) | tree_core) + tree_slot
            chosen = lax.dynamic_index_in_dim(all_ids, owner_tree, 0, keepdims=False)
            sent.append(lax.dynamic_index_in_dim(value, chosen, 0, keepdims=False))
        return jnp.stack(sent)

    got_inner = to_trees(adapter_inner)
    got_model = to_trees(jnp.concatenate([adapter_model, adapter_project], axis=1))
    got_ff = to_trees(jnp.concatenate([jnp.swapaxes(adapter_hidden, 1, 2), adapter_swiglu], axis=1))
    padded_forget = jnp.pad(forget_weight, ((0, 0), (0, EXTRA - H)))
    shards = (mixer_weight, padded_forget, output_weight, down_weight, swiglu_weight)
    x, dy = spread(tokens), spread(cotangent)
    got_inner, got_model, got_ff = (
        lax.all_to_all(v, "dp", 0, 0, tiled=True) for v in (got_inner, got_model, got_ff)
    )
    w_mix, w_forget, w_out, w_down, w_swiglu = (lax.all_gather(v, "dp", axis=0, tiled=True) for v in shards)
    inner_sel = got_inner.reshape(D, 8 * RANK)
    model_sel = jnp.swapaxes(got_model, 0, 1).reshape(6 * RANK, D)
    ff_sel = jnp.swapaxes(got_ff, 0, 1).reshape(3 * RANK, FF)
    forget_sel = lax.dynamic_slice_in_dim(forget_all, which * RANK, RANK, 0)

    zero = functools.partial(jnp.zeros, dtype=bf16)
    b_q, b_k, b_v, b_g, b_down, b_project = (model_sel[i * RANK : (i + 1) * RANK] for i in range(6))
    none = zero((RANK, D))
    line = lambda *blocks: jnp.concatenate(blocks, axis=1)
    extra_mix = jnp.concatenate(
        [
            line(b_q, none, none, none),
            line(none, b_k, none, none),
            line(none, none, b_v, none),
            line(none, none, none, b_g),
            zero((EXTRA - 4 * RANK, 4 * D)),
        ],
        axis=0,
    )
    a_in = inner_sel[:, : 5 * RANK]
    a_project = inner_sel[:, 5 * RANK : 6 * RANK]
    a_swiglu = inner_sel[:, 6 * RANK :]
    inputs = x.astype(f32)
    first_norm = (inputs * rms_scale(inputs) * attention_gain).astype(bf16)
    inner_low = linear(first_norm, a_in).astype(bf16)
    group = lambda v, i: v[:, i * RANK : (i + 1) * RANK]
    pad_low = lambda v: jnp.pad(v, ((0, 0), (0, EXTRA - v.shape[1])))
    low_pad = pad_low(inner_low)
    zero_row = jnp.zeros((1, 4 * D), f32)
    mix = lambda first, count, dtype: forward_mm(first_norm, low_pad, w_mix, extra_mix, zero_row, first, count, 512, dtype)
    forget_logit = (
        linear(first_norm, w_forget)[:, :H] + linear(group(inner_low, 4), forget_sel) + forget_bias
    ).astype(bf16)
    kv = mix(3, 6, bf16)
    kv2 = swap(kv, 1)
    forget2 = swap(forget_logit, 1)
    keys, values = kv[:, :D], kv[:, D:]
    keys2, values2 = kv2[:, :D], kv2[:, D:]
    queries = mix(0, 3, bf16)
    gate_logit = mix(9, 3, f32)

    table = jnp.array([[0, 3, 4, 7], [1, 2, 5, 6]], dtype=jnp.int32)
    mine_ids = lax.dynamic_index_in_dim(table, core, 0, keepdims=False)
    ids = jnp.concatenate([mine_ids, lax.dynamic_index_in_dim(table, 1 - core, 0, keepdims=False)])
    block = jnp.arange(8, dtype=jnp.int32)
    trunk = (block[None, :] < 4) & (block[None, :] <= block[:, None])
    reach = trunk | (block[:, None] == block[None, :]) | (
        (block[:, None] >= 4) & (block[None, :] >= 4) & (parent_row[:, None] == block[None, :])
    )
    strict = (reach & (block[:, None] != block[None, :])).astype(f32)
    pick = (ids[:, None] == block[None, :]).astype(f32)
    strict_local = jnp.dot(jnp.dot(pick, strict, precision=highest), pick.T, precision=highest)
    spot_of = jnp.array([0, 4, 5, 1, 2, 6, 7, 3], dtype=jnp.int32) ^ (4 * core)
    first_entries = jnp.where(
        core == 0,
        jnp.array([-1, 0, 0, 1, 2, 3], dtype=jnp.int32),
        jnp.array([0, 1, 0, 1, -1, 2], dtype=jnp.int32),
    )
    tails = []
    for place in (2, 3):
        own = mine_ids[place]
        up = parent_row[own]
        up = jnp.where(up >= 4, up, -1)
        tails.append(jnp.concatenate([jnp.arange(4, dtype=jnp.int32), up[None], own[None]]))
    entries = jnp.concatenate([first_entries] + tails)
    valid = entries >= 0
    where = jnp.where(valid, spot_of[jnp.maximum(entries, 0)], 0).astype(jnp.int32)

    logits_all = jnp.concatenate([forget_logit, forget2], axis=0).astype(f32)
    log_forget = jax.nn.log_sigmoid(logits_all).T.reshape(H, 8, BLOCK)
    upper = (jnp.arange(BLOCK)[:, None] <= jnp.arange(BLOCK)[None, :]).astype(f32)
    within = jnp.dot(log_forget, upper, precision=highest)
    offsets = jnp.dot(within[:, :, BLOCK - 1], strict_local.T, precision=highest)
    path_sum = within + offsets[:, :, None]
    bias = jnp.where(valid[None, :, None], -path_sum[:, where], -1e30)
    bias = bias.reshape(PAIRS, 2, TOTAL * BLOCK)

    attended, probs = attend(where, queries, keys, values, keys2, values2, bias)
    gate_open = jax.nn.sigmoid(gate_logit)
    gated = (attended * gate_open).astype(bf16)
    project_low = linear(gated, a_project).astype(bf16)
    extra_out = jnp.pad(b_project, ((0, EXTRA - RANK), (0, 0)))
    out = forward_mm(gated, pad_low(project_low), w_out, extra_out, zero_row, 0, 3, 512, f32)
    middle = inputs + out
    second_norm = (middle * rms_scale(middle) * feedforward_gain).astype(bf16)
    swiglu_low = linear(second_norm, a_swiglu).astype(bf16)
    lowg, lowu = swiglu_low[:, :RANK], swiglu_low[:, RANK:]

    hidden_low_grad = linear_back(dy, b_down).astype(bf16)
    second_out, down_out, slg, slu, hidden_low, ff_pack = swiglu(
        second_norm, lowg, lowu, dy, hidden_low_grad, w_swiglu,
        ff_sel[RANK : 2 * RANK], ff_sel[2 * RANK :], w_down, ff_sel[:RANK],
    )
    hidden_low = hidden_low.astype(bf16)
    result = (middle + down_out + linear(hidden_low, b_down)).astype(bf16)
    outputs = collect(result)

    swiglu_low_grad = jnp.concatenate([slg, slu], axis=1).astype(bf16)
    second_grad = second_out + linear_back(swiglu_low_grad, a_swiglu)
    middle_grad = dy.astype(f32) + norm_back(middle, feedforward_gain, second_grad)
    branch_grad = middle_grad.astype(bf16)
    project_low_grad = linear_back(branch_grad, b_project).astype(bf16)
    none_low = jnp.zeros((rows, EXTRA), f32)
    gated_grad = backward_mm(
        branch_grad, w_out, zero((EXTRA, D)), 0, 3, 512, linear_back(project_low_grad, a_project), none_low
    )[0]
    attended_grad = (gated_grad * gate_open).astype(bf16)
    gate_logit_grad = (gated_grad * attended * gate_open * (1.0 - gate_open)).astype(bf16)

    dq, dk_all, dv_all, query_sum, key_sum = attend_back(
        where, queries, keys, values, keys2, values2, attended_grad, attended, probs
    )
    inner_g_grad = linear_back(gate_logit_grad, b_g).astype(bf16)
    early = jnp.concatenate(
        [
            linear_grad(gated, project_low_grad),
            linear_grad(second_norm, swiglu_low_grad),
            linear_grad(first_norm, inner_g_grad),
            linear_grad(dy, hidden_low),
            linear_grad(branch_grad, project_low),
            linear_grad(gate_logit_grad, group(inner_low, 3)),
            jnp.zeros((D, RANK), f32),
        ],
        axis=1,
    ).astype(bf16).reshape(dp, wide, 128)
    ff_pack = jnp.swapaxes(ff_pack.reshape(3 * RANK, dp, tall), 0, 1)
    theirs = jnp.concatenate([dk_all[rows:], dv_all[rows:]], axis=1)
    back = swap(theirs, 1)
    key_sum = jnp.swapaxes(key_sum, 0, 1)[:H]
    query_part = query_sum[:, :H].T.reshape(H, 4, BLOCK)
    decay = jnp.concatenate([query_part - key_sum[:, :4], -key_sum[:, 4:]], axis=1)
    other = swap(decay, 1)
    decay = decay + jnp.concatenate([other[:, 4:], other[:, :4]], axis=1)
    suffix = jnp.dot(decay[:, :4], upper.T, precision=highest)
    below = jnp.dot(jnp.sum(decay, axis=2), strict_local[:, :4], precision=highest)
    logf_grad = (suffix + below[:, :, None]).reshape(H, rows).T
    forget_grad_low = (logf_grad * jax.nn.sigmoid(-forget_logit.astype(f32))).astype(bf16)
    dk = (dk_all[:rows].astype(f32) + back[:, :D].astype(f32)).astype(bf16)
    dv = (dv_all[:rows].astype(f32) + back[:, D:].astype(f32)).astype(bf16)
    first_out, first_low = backward_mm(
        jnp.concatenate([dq, dk, dv, gate_logit_grad], axis=1), w_mix, extra_mix, 0, 12, 512,
        jnp.zeros((rows, D), f32), none_low,
    )
    inner_low_grad = jnp.concatenate(
        [first_low[:, : 4 * RANK], linear_back(forget_grad_low, forget_sel)], axis=1
    ).astype(bf16)
    first_grad = first_out + linear_back(inner_low_grad, a_in) + linear_back(pad_low(forget_grad_low), w_forget)
    input_grad = middle_grad + norm_back(inputs, attention_gain, first_grad)
    input_grads = collect(input_grad.astype(bf16)).astype(f32)
    forget_piece = linear_grad(forget_grad_low, group(inner_low, 4))
    forget_slab = jnp.broadcast_to(jnp.pad(forget_piece, ((0, -H % wide), (0, 0)))[None, :wide], (dp, wide, RANK))
    late = jnp.concatenate(
        [
            linear_grad(first_norm, inner_low_grad[:, : 3 * RANK]),
            linear_grad(first_norm, inner_low_grad[:, 4 * RANK :]),
            linear_grad(dq, group(inner_low, 0)),
            linear_grad(dk, group(inner_low, 1)),
            linear_grad(dv, group(inner_low, 2)),
        ],
        axis=1,
    ).reshape(dp, wide, 7 * RANK)
    late = jnp.concatenate([late, forget_slab], axis=2).astype(bf16)

    def to_owners(value):
        taken = lax.all_to_all(value, "dp", 0, 0, tiled=True)
        trees = jnp.sum(taken.astype(f32).reshape((dp // 2, 2) + value.shape[1:]), axis=1).astype(bf16)
        found = [trees]
        for k in (1, 2, 3):
            found.append(lax.ppermute(trees, "seq", [(i, i ^ k) for i in range(4)]))
        return jnp.concatenate(found, axis=0)

    ff_trees, early_trees, late_trees = to_owners(ff_pack), to_owners(early), to_owners(late)

    chip = jnp.arange(dp // 2, dtype=jnp.int32)
    at = jnp.arange(seq, dtype=jnp.int32) ^ z
    tree_of = 2 * (2 * chip[None, :] + (at >> 1)[:, None]) + (at & 1)[:, None]
    id_of = all_ids[tree_of.reshape(-1)]
    one_hot = (jnp.arange(ADAPTERS, dtype=jnp.int32)[:, None] == id_of[None, :]).astype(bf16)

    def by_adapter(value):
        return jnp.einsum("at,trc->arc", one_hot, value, preferred_element_type=f32)

    ff_sum, early_sum, late_sum = by_adapter(ff_trees), by_adapter(early_trees), by_adapter(late_trees)
    turned = lambda v: jnp.swapaxes(v, 1, 2)
    at16 = lambda v, i, n=1: v[:, :, i * RANK : (i + n) * RANK]
    per = ADAPTERS * RANK // dp
    forget_sum = turned(at16(late_sum, 7)[:, :H]).reshape(ADAPTERS * RANK, H)
    return (
        outputs,
        input_grads,
        jnp.concatenate(
            [at16(late_sum, 0, 3), at16(early_sum, 3), at16(late_sum, 3), at16(early_sum, 0, 3)], axis=2
        ),
        turned(ff_sum[:, :RANK]),
        turned(jnp.concatenate([at16(late_sum, 4, 3), at16(early_sum, 6), at16(early_sum, 4)], axis=2)),
        turned(at16(early_sum, 5)),
        ff_sum[:, RANK:],
        lax.dynamic_slice_in_dim(forget_sum, me * per, per, 0),
    )


def solution(mesh):
    paired = mesh.shape["dp"] == 8 and mesh.shape["seq"] == 4
    placed = (
        P("dp", "seq", None),
        P("dp", "seq", None),
        P("dp", None),
        P("dp"),
        P(),
        P("dp", None),
        P("dp", None),
        P(),
        P("dp", None),
        P(),
        P("dp", None),
        P("dp", None),
        P(None, "dp", None),
        P(None, "dp", None),
        P(None, None, "dp"),
        P(None, None, "dp"),
        P(None, None, "dp"),
        P("dp", None),
    )
    return jax.shard_map(
        body_paired if paired else functools.partial(body_plain, (mesh.shape["dp"], mesh.shape["seq"])),
        mesh=mesh,
        in_specs=placed,
        out_specs=(
            P("dp", "seq", None),
            P("dp", "seq", None),
            P(None, "dp", None),
            P(None, "dp", None),
            P(None, None, "dp"),
            P(None, None, "dp"),
            P(None, None, "dp"),
            P("dp", None),
        ),
        check_vma=False,
    )
```
